256 devices in a mesh: site: 16 (over z_hi, y, core), blk: 16 (over z_lo, x).
Axes of the slice: x: 4, y: 4, z: 8 (z_hi: 2, z_lo: 4; z = z_hi * 4 + z_lo), core: 2. Of those that a mesh axis runs over, the one named last changes fastest.
Arguments:
- corner: bfloat16 [16, 96, 128, 128], P('site', 'blk')
- bcorner: bfloat16 [2, 16, 96, 128, 128], P(None, 'site', 'blk'), may hold values from -6 to 6
- edge: bfloat16 [16, 96, 128, 2304], P('site', 'blk'), may hold values from -0.5 to 0.5
- bedge: bfloat16 [16, 96, 128, 2304], P('site', 'blk'), may hold values from -0.5 to 0.5
- proj: bfloat16 [16, 96, 2304, 128], P('site', 'blk'), may hold values from -0.125 to 0.125
- joining: int32 [16, 96], P('site'), may hold values from 0 to 95, as said below
- momentum: float32 [1], replicated, may hold values from 0.5 to 2.5
Outputs:
- new_corner: bfloat16 [16, 96, 128, 128], P('site', 'blk')
- new_bcorner: bfloat16 [2, 16, 96, 128, 128], P(None, 'site', 'blk')
- momentum_sum: float32 [2, 96, 128, 128], P(None, 'blk', 'site')
The draws below stay inside these ranges and needn't reach their ends.
Inputs may be any that keep to these rules, and one draw needn't show every extreme that they name: Each row of joining is a permutation of the 96 slots. The 6 new slots of one blk device take their blocks from the slots of at most 3 blk devices, exactly 2 from each of them.
All inputs are finite; a program needn't handle non-finite values. Where the reference program divides by a largest or mean magnitude, that divisor is 1e-20 or more.
Results may differ from the reference program's by a relative error of at most 0.024.
Values may be sent and summed in bfloat16 or wider, within the bound.
A program may use at most 128 MiB of HBM per device.

```python
import jax
import jax.numpy as jnp
from jax import lax

M = 128
K = 2304
CAP = 2
NB_DEV = 6
SITES = 16
SLOTS = 96


def draw_corner(key, part):
    key_base, key_rows, key_cols = jax.random.split(jax.random.fold_in(key, 11), 3)
    base = jax.random.normal(key_base, (SITES, SLOTS, M, M), jnp.float32)
    rows = jnp.exp((jax.random.uniform(key_rows, (SITES, SLOTS, M, 1), jnp.float32) - 0.5) * jnp.log(10.0))
    cols = jnp.exp((jax.random.uniform(key_cols, (SITES, SLOTS, 1, M), jnp.float32) - 0.5) * jnp.log(10.0))
    slot_scale = 1.0 + 2.0 * jnp.arange(SLOTS, dtype=jnp.float32) / max(SLOTS - 1, 1)
    return (base * rows * cols * slot_scale[None, :, None, None]).astype(jnp.bfloat16)


def joining_site(key):
    groups = NB_DEV // CAP
    blocks = SLOTS // NB_DEV
    key_off, key_src, key_dst = jax.random.split(key, 3)
    offsets = jax.random.permutation(key_off, blocks)[:groups]
    shuffle_src = jax.vmap(lambda subkey: jax.random.permutation(subkey, NB_DEV))(jax.random.split(key_src, blocks))
    shuffle_dst = jax.vmap(lambda subkey: jax.random.permutation(subkey, NB_DEV))(jax.random.split(key_dst, blocks))
    targets = jnp.arange(blocks, dtype=jnp.int32)[:, None]
    positions = jnp.arange(NB_DEV, dtype=jnp.int32)[None, :]
    group_of = positions // CAP
    within = positions % CAP
    source_device = (targets + offsets[group_of]) % blocks
    source_slot = shuffle_src[source_device, group_of * CAP + within]
    sources = source_device * NB_DEV + source_slot
    shuffled = jnp.take_along_axis(sources, shuffle_dst, axis=1)
    return shuffled.reshape(SLOTS).astype(jnp.int32)


def draw_joining(key, part):
    keys = jax.random.split(jax.random.fold_in(key, 23), SITES)
    return jax.vmap(joining_site)(keys)


def level_of(stream_key, extent, cuts, low, top_value):
    factor_of = 1.0
    for dim, shards_of in cuts:
        steps = jax.random.uniform(jax.random.fold_in(jax.random.fold_in(stream_key, 6), dim), (shards_of,), jnp.float32, low / len(cuts), top_value / len(cuts))
        factor_of = factor_of * jnp.repeat(jnp.exp(steps), extent[dim] // shards_of).reshape((-1,) + (1,) * (len(extent) - 1 - dim))
    return factor_of


def normal_values(own_key, extent, spread, limit, pieces=(), kind=jnp.bfloat16):
    factor_of = level_of(own_key, extent, pieces, -0.22, 0.18) if pieces else 1.0
    array = jax.random.normal(own_key, extent, jnp.float32) * spread * factor_of
    return jnp.minimum(jnp.maximum(array, -limit), limit).astype(kind)


def setup_inputs(seed: int = 0) -> dict:
    seeds = jax.random.split(jax.random.key(seed), 8)
    return {
        "corner": draw_corner(jax.random.fold_in(seeds[7], 71), 0),
        "bcorner": normal_values(seeds[1], (2, SITES, SLOTS, M, M), 1.0, 6.0, ((1, 16), (2, 16))),
        "edge": normal_values(seeds[2], (SITES, SLOTS, M, K), M ** -0.5, 0.5, ((0, 16), (1, 16))),
        "bedge": normal_values(seeds[3], (SITES, SLOTS, M, K), M ** -0.5, 0.5, ((0, 16), (1, 16))),
        "proj": normal_values(seeds[4], (SITES, SLOTS, K, M), K ** -0.5, 0.125, ((0, 16), (1, 16))),
        "joining": draw_joining(jax.random.fold_in(seeds[7], 71), 0),
        "momentum": jnp.clip(jax.random.uniform(seeds[6], (1,), jnp.float32, 0.5, 2.5), 0.5, 2.5),
    }


epsilon = 1e-6


def product(left, right):
    return jnp.einsum("jmn,jnk->jmk", left.astype(jnp.float32), right.astype(jnp.float32), precision=lax.Precision.HIGHEST)


def reference(corner, bcorner, edge, bedge, proj, joining, momentum):
    left_corner = jnp.roll(corner, 1, axis=0)
    left_bcorner = jnp.moveaxis(jnp.roll(bcorner, 1, axis=1), 0, 1)
    sites = jnp.arange(SITES, dtype=jnp.int32)

    def one_site(items):
        corner_here, bcorner_here, column, bcolumn, project, sources, index = items
        enlarged = product(corner_here, column).astype(jnp.bfloat16)
        real_term = product(bcorner_here[0], column)
        imag_term = product(bcorner_here[1], column)
        inserted = product(corner_here, bcolumn)
        angle = momentum[0] * index.astype(jnp.float32)
        cosine = jnp.cos(angle)
        sine = jnp.sin(angle)
        excited_re = (cosine * real_term - sine * imag_term + inserted).astype(jnp.bfloat16)
        excited_im = (sine * real_term + cosine * imag_term).astype(jnp.bfloat16)
        projected = jnp.stack([product(enlarged, project).astype(jnp.bfloat16),
                               product(excited_re, project).astype(jnp.bfloat16),
                               product(excited_im, project).astype(jnp.bfloat16)], axis=1)
        peak = jnp.max(jnp.abs(projected[:, 0].astype(jnp.float32)))
        routed = projected[sources]
        scaled = routed.astype(jnp.float32) / (peak + epsilon)
        new_corner = scaled[:, 0].astype(jnp.bfloat16)
        new_b = jnp.stack([scaled[:, 1], scaled[:, 2]], axis=0).astype(jnp.bfloat16)
        return new_corner, new_b

    corners, bparts = lax.map(one_site, (left_corner, left_bcorner, edge, bedge, proj, joining, sites))
    new_bcorner = jnp.moveaxis(bparts, 0, 1)
    momentum_sum = jnp.sum(new_bcorner.astype(jnp.float32), axis=1)
    return corners, new_bcorner, momentum_sum
```

```python
import functools

import jax
import jax.numpy as jnp
from jax import lax
from jax.experimental import pallas as pl
from jax.experimental.pallas import tpu as pltpu
from jax.sharding import PartitionSpec as P

EPS = 1e-6
MESH = pl.DeviceIdType.MESH
NX = 4
NZ = 4
BLOCKS = 3
ORDER = (1, 2, 0)
HALVES = 2


def mega(
    n_site,
    join_ref,
    mom_ref,
    corner_ref,
    bcorner_ref,
    edge_ref,
    bedge_ref,
    proj_ref,
    outc_ref,
    outb_ref,
    sum_ref,
    edge_v,
    bedge_v,
    proj_v,
    cb_v,
    e_v,
    d_v,
    peak_src,
    peak_all,
    msend,
    mrecv,
    tab,
    *rest,
):
    nb = edge_v.shape[0]
    m = cb_v.shape[-1]
    n_blk = NX * NZ
    rows = m // HALVES
    chunks = [(b, h) for b in ORDER for h in range(HALVES)]
    nc = len(chunks)
    gath = rest[:nc]
    xsend = rest[nc : 2 * nc]
    got = rest[2 * nc : 3 * nc]
    (load_sem, s_send, s_recv, z_up, z_down, z_recv, x_send, x_recv, p_send, p_recv, m_send, m_recv) = rest[
        3 * nc :
    ]

    site = lax.axis_index("site")
    blk = lax.axis_index("blk")
    z = blk // NX
    x = blk % NX

    def at(s, b):
        return {"site": s, "blk": b}

    barrier = pltpu.get_barrier_semaphore()
    for k in range(1, n_site):
        pl.semaphore_signal(barrier, inc=1, device_id=at((site + k) % n_site, blk), device_id_type=MESH)
    for k in range(1, n_blk):
        pl.semaphore_signal(barrier, inc=1, device_id=at(site, (blk + k) % n_blk), device_id_type=MESH)

    def loads(q):
        return [
            pltpu.make_async_copy(src.at[0, q], dst.at[q], load_sem.at[i, q])
            for i, (src, dst) in enumerate(((edge_ref, edge_v), (bedge_ref, bedge_v), (proj_ref, proj_v)))
        ]

    for q in range(nb):
        for copy in loads(q):
            copy.start()

    for dx in range(NX):
        target = z * NX + (x + dx) % NX
        for k in range(nb):
            src = join_ref[0, target * nb + k]
            dev = src // nb
            tab[dx * nb + k] = (dev // NX) * nb + (src - dev * nb)
            if dx == 0:
                tab[NX * nb + k] = (x - dev % NX + NX) % NX

    pl.semaphore_wait(barrier, n_site + n_blk - 2)

    right = (site + 1) % n_site
    shift = [
        pltpu.make_async_remote_copy(
            src_ref=corner_ref.at[0],
            dst_ref=cb_v.at[0],
            send_sem=s_send.at[0],
            recv_sem=s_recv.at[0],
            device_id=at(right, blk),
            device_id_type=MESH,
        )
    ] + [
        pltpu.make_async_remote_copy(
            src_ref=bcorner_ref.at[c, 0],
            dst_ref=cb_v.at[1 + c],
            send_sem=s_send.at[1 + c],
            recv_sem=s_recv.at[1 + c],
            device_id=at(right, blk),
            device_id_type=MESH,
        )
        for c in range(2)
    ]
    for copy in shift:
        copy.start()

    def local(q, carry):
        for copy in loads(q):
            copy.wait()
        both = jnp.concatenate([edge_v[q], bedge_v[q]], axis=0)
        prod = jnp.dot(both, proj_v[q], preferred_element_type=jnp.float32).astype(jnp.bfloat16)
        e_v[q] = prod[:m]
        d_v[q] = prod[m:]
        return carry

    lax.fori_loop(0, nb, local, 0)

    angle = jnp.full((8, m), mom_ref[0] * site.astype(jnp.float32), jnp.float32)
    cosine = jnp.cos(angle)[:1]
    sine = jnp.sin(angle)[:1]

    for copy in shift:
        copy.wait_recv()

    def join_slot(q, top):
        left = jnp.concatenate([cb_v[0, q], cb_v[1, q], cb_v[2, q]], axis=0)
        main = jnp.dot(left, e_v[q], preferred_element_type=jnp.float32)
        inserted = jnp.dot(cb_v[0, q], d_v[q], preferred_element_type=jnp.float32)
        real, imag = main[m : 2 * m], main[2 * m :]
        blocks = [
            main[:m].astype(jnp.bfloat16),
            (cosine * real - sine * imag + inserted).astype(jnp.bfloat16),
            (sine * real + cosine * imag).astype(jnp.bfloat16),
        ]
        for c, (b, h) in enumerate(chunks):
            gath[c][z * nb + q] = blocks[b][h * rows : (h + 1) * rows]
        return jnp.maximum(top, jnp.max(jnp.abs(blocks[0].astype(jnp.float32))))

    top = lax.fori_loop(0, nb, join_slot, jnp.float32(0.0))
    peak_src[...] = jnp.full(peak_src.shape, top, jnp.float32)

    peaks = [
        pltpu.make_async_remote_copy(
            src_ref=peak_src,
            dst_ref=peak_all.at[k - 1],
            send_sem=p_send.at[k - 1],
            recv_sem=p_recv.at[k - 1],
            device_id=at(site, (blk + k) % n_blk),
            device_id_type=MESH,
        )
        for k in range(1, n_blk)
    ]

    def hop(c, j, up):
        sems = z_up if up else z_down
        step = z - j if up else j - z
        view = gath[c].at[pl.ds(j * nb, nb)]
        return pltpu.make_async_remote_copy(
            src_ref=view,
            dst_ref=view,
            send_sem=sems.at[c, step],
            recv_sem=z_recv.at[c, j],
            device_id=at(site, blk + NX if up else blk - NX),
            device_id_type=MESH,
        )

    def relay(c, s):
        @pl.when(z - s >= 0)
        def _():
            if s > 0:
                hop(c, z - s, True).wait_recv()

            if s < NZ - 1:

                @pl.when(z < NZ - 1)
                def _():
                    hop(c, z - s, True).start()

        @pl.when(z + s <= NZ - 1)
        def _():
            if s > 0:
                hop(c, z + s, False).wait_recv()

            if s < NZ - 1:

                @pl.when(z > 0)
                def _():
                    hop(c, z + s, False).start()

    def cross(c, dx):
        return pltpu.make_async_remote_copy(
            src_ref=xsend[c].at[dx - 1],
            dst_ref=got[c].at[dx],
            send_sem=x_send.at[c, dx - 1],
            recv_sem=x_recv.at[c, dx - 1],
            device_id=at(site, z * NX + (x + dx) % NX),
            device_id_type=MESH,
        )

    def send_x(c):
        for dx in (2, 1, 3):
            for k in range(nb):
                xsend[c][dx - 1, k] = gath[c][tab[dx * nb + k]]
            cross(c, dx).start()
        for k in range(nb):
            got[c][0, k] = gath[c][tab[k]]

    state = {}

    def finish(c):
        b, h = chunks[c]
        for dx in (2, 1, 3):
            cross(c, dx).wait_recv()
        if "scale" not in state:
            for copy in peaks:
                copy.wait_recv()
            best = peak_src[...]
            for k in range(n_blk - 1):
                best = jnp.maximum(best, peak_all[k])
            state["scale"] = best[:1] + EPS
        scale = state["scale"]
        held = []
        for k in range(nb):
            value = got[c][tab[NX * nb + k], k].astype(jnp.float32) / scale
            if b == 0:
                outc_ref[0, k, pl.ds(h * rows, rows)] = value.astype(jnp.bfloat16)
            else:
                outb_ref[b - 1, 0, k, pl.ds(h * rows, rows)] = value.astype(jnp.bfloat16)
                held.append(value.reshape(rows // 8, 8, m))
        for j in range(len(held) // 2):
            pair = jnp.concatenate([held[2 * j], held[2 * j + 1]], axis=1)
            msend[b - 1, pl.ds(h * (rows // 8), rows // 8), j] = pair.astype(jnp.bfloat16)

    def spread(c, k):
        return pltpu.make_async_remote_copy(
            src_ref=msend.at[c, (site + k) % n_site],
            dst_ref=mrecv.at[c, k - 1],
            send_sem=m_send.at[c, k - 1],
            recv_sem=m_recv.at[c, k - 1],
            device_id=at((site + k) % n_site, blk),
            device_id_type=MESH,
        )

    for step in range(nc + NZ):
        for c in range(nc):
            stage = step - c
            if 0 <= stage < NZ:
                relay(c, stage)
                if stage == NZ - 1:
                    send_x(c)
            elif stage == NZ:
                finish(c)
                b, h = chunks[c]
                if b > 0 and h == HALVES - 1:
                    for k in (8, 7, 9, 6, 10, 5, 11, 4, 12, 3, 13, 2, 14, 1, 15):
                        spread(b - 1, k).start()
        if step == 0:
            for copy in peaks:
                copy.start()

    for c in range(2):
        total = msend[c, site].astype(jnp.float32)
        for k in range(1, n_site):
            spread(c, k).wait_recv()
            total = total + mrecv[c, k - 1].astype(jnp.float32)
        for j in range(nb // 2):
            sum_ref[c, 2 * j] = total[j, :8]
            sum_ref[c, 2 * j + 1] = total[j, 8:]

    for copy in shift:
        copy.wait_send()
    for copy in peaks:
        copy.wait_send()
    for c in range(nc):
        for s in range(NZ - 1):

            @pl.when(jnp.logical_and(z - s >= 0, z < NZ - 1))
            def _():
                hop(c, z - s, True).wait_send()

            @pl.when(jnp.logical_and(z + s <= NZ - 1, z > 0))
            def _():
                hop(c, z + s, False).wait_send()

        for dx in (1, 2, 3):
            cross(c, dx).wait_send()
    for c in range(2):
        for k in range(1, n_site):
            spread(c, k).wait_send()


def per_device(n_site, corner, bcorner, edge, bedge, proj, joining, momentum):
    _, nb, m, kdim = edge.shape
    rows = m // HALVES
    n_blk = NX * NZ
    nc = BLOCKS * HALVES
    bf = jnp.bfloat16
    hbm = pl.BlockSpec(memory_space=pl.ANY)
    smem = pl.BlockSpec(memory_space=pltpu.SMEM)
    vmem = pl.BlockSpec(memory_space=pltpu.VMEM)
    dma = pltpu.SemaphoreType.DMA
    return pl.pallas_call(
        functools.partial(mega, n_site),
        out_shape=(
            jax.ShapeDtypeStruct(corner.shape, bf),
            jax.ShapeDtypeStruct(bcorner.shape, bf),
            jax.ShapeDtypeStruct((2, nb, m // n_site, m), jnp.float32),
        ),
        in_specs=[smem, smem, hbm, hbm, hbm, hbm, hbm],
        out_specs=(vmem, vmem, vmem),
        scratch_shapes=[
            pltpu.VMEM((nb, m, kdim), bf),
            pltpu.VMEM((nb, m, kdim), bf),
            pltpu.VMEM((nb, kdim, m), bf),
            pltpu.VMEM((3, nb, m, m), bf),
            pltpu.VMEM((nb, m, m), bf),
            pltpu.VMEM((nb, m, m), bf),
            pltpu.VMEM((8, m), jnp.float32),
            pltpu.VMEM((n_blk - 1, 8, m), jnp.float32),
            pltpu.VMEM((2, n_site, nb // 2, 16, m), bf),
            pltpu.VMEM((2, n_site - 1, nb // 2, 16, m), bf),
            pltpu.SMEM(((NX + 1) * nb,), jnp.int32),
        ]
        + [pltpu.VMEM((NZ * nb, rows, m), bf)] * nc
        + [pltpu.VMEM((NX - 1, nb, rows, m), bf)] * nc
        + [pltpu.VMEM((NX, nb, rows, m), bf)] * nc
        + [
            dma((3, nb)),
            dma((3,)),
            dma((3,)),
            dma((nc, NZ - 1)),
            dma((nc, NZ - 1)),
            dma((nc, NZ)),
            dma((nc, NX - 1)),
            dma((nc, NX - 1)),
            dma((n_blk - 1,)),
            dma((n_blk - 1,)),
            dma((2, n_site - 1)),
            dma((2, n_site - 1)),
        ],
        compiler_params=pltpu.CompilerParams(
            collective_id=0, has_side_effects=True, vmem_limit_bytes=48 << 20
        ),
        name="column_move",
    )(joining, momentum, corner, bcorner, edge, bedge, proj)


def solution(mesh):
    in_specs = (
        P("site", "blk", None, None),
        P(None, "site", "blk", None, None),
        P("site", "blk", None, None),
        P("site", "blk", None, None),
        P("site", "blk", None, None),
        P("site", None),
        P(),
    )
    out_specs = (
        P("site", "blk", None, None),
        P(None, "site", "blk", None, None),
        P(None, "blk", "site", None),
    )
    return jax.shard_map(
        functools.partial(per_device, mesh.shape["site"]),
        mesh=mesh,
        in_specs=in_specs,
        out_specs=out_specs,
        check_vma=False,
    )
```

```python
import functools

import jax
import jax.numpy as jnp
from jax import lax
from jax.experimental import pallas as pl
from jax.experimental.pallas import tpu as pltpu
from jax.sharding import PartitionSpec as P

EPS = 1e-6
MESH = pl.DeviceIdType.MESH
NX = 4
NZ = 4
HALVES = 2
CHUNKS = (
    (True, 0, (1, 2)),
    (False, 1, (1, 2)),
    (True, 0, (0,)),
    (False, 1, (0,)),
)


def mega(
    n_site,
    join_ref,
    mom_ref,
    corner_ref,
    bcorner_ref,
    edge_ref,
    bedge_ref,
    proj_ref,
    outc_ref,
    outb_ref,
    sum_ref,
    edge_v,
    bedge_v,
    proj_v,
    cb_v,
    e_v,
    d_v,
    peak_src,
    peak_x,
    peak_mid,
    peak_z,
    msend,
    mrecv,
    mpart,
    mcross,
    tab,
    jsm,
    *rest,
):
    nb = edge_v.shape[0]
    m = cb_v.shape[-1]
    rows = m // HALVES
    nc = len(CHUNKS)
    along_z = [chunk[0] for chunk in CHUNKS]
    n_near = n_site // 2
    gath = rest[:nc]
    parts = [rest[nc + 5 * i : nc + 5 * i + 5] for i in range(nc)]
    (load_sem, s_send, s_recv, z_up, z_down, z_recv, x_send, x_recv, up_send, up_recv, dn_send, dn_recv, p_send, p_recv, m_send, m_recv, c_send, c_recv, j_sem) = rest[
        6 * nc :
    ]

    site = lax.axis_index("site")
    blk = lax.axis_index("blk")
    z = blk // NX
    x = blk % NX

    def at(s, b):
        return {"site": s, "blk": b}

    barrier = pltpu.get_barrier_semaphore()
    near, far = site % n_near, site // n_near

    def mate(k):
        return at(far * n_near + (near + k) % n_near, blk)

    def row_mate(dx):
        return at(site, z * NX + (x + dx) % NX)

    def column_mate(dz):
        return at(site, (z + dz) % NZ * NX + x)

    right, left = at((site + 1) % n_site, blk), at((site + n_site - 1) % n_site, blk)
    across = at((site + n_near) % n_site, blk)
    partners = (
        [right, left, across]
        + [mate(k) for k in range(1, n_near)]
        + [row_mate(d) for d in range(1, NX)]
        + [column_mate(d) for d in range(1, NZ)]
    )
    for partner in partners:
        pl.semaphore_signal(barrier, inc=1, device_id=partner, device_id_type=MESH)

    def loads(q):
        return [
            pltpu.make_async_copy(src.at[0, q], dst.at[q], load_sem.at[i, q])
            for i, (src, dst) in enumerate(((edge_ref, edge_v), (bedge_ref, bedge_v), (proj_ref, proj_v)))
        ]

    fetch = pltpu.make_async_copy(join_ref, jsm, j_sem)
    fetch.start()
    for q in range(nb):
        for copy in loads(q):
            copy.start()

    base = (NX + 1) * nb
    fetch.wait()
    for dx in range(NX):
        target = z * NX + (x + dx) % NX
        for k in range(nb):
            src = jsm[0, target * nb + k]
            dev = src // nb
            tab[dx * nb + k] = (dev // NX) * nb + (src - dev * nb)
            if dx == 0:
                tab[NX * nb + k] = (x - dev % NX + NX) % NX
    for t in range(NZ):
        for k in range(nb):
            src = jsm[0, (t * NX + x) * nb + k]
            dev = src // nb
            tab[base + t * nb + k] = (dev % NX) * nb + (src - dev * nb)
            tab[base + (NZ + t) * nb + k] = dev // NX

    pl.semaphore_wait(barrier, len(partners))

    def shift(h):
        part = pl.ds(h * rows, rows)
        sources = [corner_ref.at[0, :, part]] + [bcorner_ref.at[c, 0, :, part] for c in range(2)]
        return [
            pltpu.make_async_remote_copy(
                src_ref=source,
                dst_ref=cb_v.at[h, c],
                send_sem=s_send.at[h, c],
                recv_sem=s_recv.at[h, c],
                device_id=right,
                device_id_type=MESH,
            )
            for c, source in enumerate(sources)
        ]

    for h in range(HALVES):
        for copy in shift(h):
            copy.start()

    def local(q, carry):
        for copy in loads(q):
            copy.wait()
        both = jnp.concatenate([edge_v[q], bedge_v[q]], axis=0)
        prod = jnp.dot(both, proj_v[q], preferred_element_type=jnp.float32).astype(jnp.bfloat16)
        e_v[q] = prod[:m]
        d_v[q] = prod[m:]
        return carry

    lax.fori_loop(0, nb, local, 0)

    angle = jnp.full((8, m), mom_ref[0] * site.astype(jnp.float32), jnp.float32)
    cosine = jnp.cos(angle)[:1]
    sine = jnp.sin(angle)[:1]

    def join(h, top):
        for copy in shift(h):
            copy.wait_recv()

        def join_slot(q, top):
            left_rows = jnp.concatenate([cb_v[h, 0, q], cb_v[h, 1, q], cb_v[h, 2, q]], axis=0)
            main = jnp.dot(left_rows, e_v[q], preferred_element_type=jnp.float32)
            inserted = jnp.dot(cb_v[h, 0, q], d_v[q], preferred_element_type=jnp.float32)
            real, imag = main[rows : 2 * rows], main[2 * rows :]
            blocks = [
                main[:rows].astype(jnp.bfloat16),
                (cosine * real - sine * imag + inserted).astype(jnp.bfloat16),
                (sine * real + cosine * imag).astype(jnp.bfloat16),
            ]
            for c, (zfirst, half, held) in enumerate(CHUNKS):
                if half == h:
                    for i, b in enumerate(held):
                        gath[c][(z if zfirst else x) * nb + q, pl.ds(i * rows, rows)] = blocks[b]
            return jnp.maximum(top, jnp.max(jnp.abs(blocks[0].astype(jnp.float32))))

        return lax.fori_loop(0, nb, join_slot, top)

    peaks_x = [
        pltpu.make_async_remote_copy(
            src_ref=peak_src,
            dst_ref=peak_x.at[d - 1],
            send_sem=p_send.at[0, d - 1],
            recv_sem=p_recv.at[0, d - 1],
            device_id=row_mate(d),
            device_id_type=MESH,
        )
        for d in range(1, NX)
    ]
    peaks_z = [
        pltpu.make_async_remote_copy(
            src_ref=peak_mid,
            dst_ref=peak_z.at[d - 1],
            send_sem=p_send.at[1, d - 1],
            recv_sem=p_recv.at[1, d - 1],
            device_id=column_mate(d),
            device_id_type=MESH,
        )
        for d in range(1, NZ)
    ]

    def hop(c, j, up):
        sems = z_up if up else z_down
        step = z - j if up else j - z
        view = gath[c].at[pl.ds(j * nb, nb)]
        return pltpu.make_async_remote_copy(
            src_ref=view,
            dst_ref=view,
            send_sem=sems.at[c, step],
            recv_sem=z_recv.at[c, j],
            device_id=at(site, blk + NX if up else blk - NX),
            device_id_type=MESH,
        )

    def relay(c, s):
        @pl.when(z - s >= 0)
        def _():
            if s > 0:
                hop(c, z - s, True).wait_recv()

            if s < NZ - 1:

                @pl.when(z < NZ - 1)
                def _():
                    hop(c, z - s, True).start()

        @pl.when(z + s <= NZ - 1)
        def _():
            if s > 0:
                hop(c, z + s, False).wait_recv()

            if s < NZ - 1:

                @pl.when(z > 0)
                def _():
                    hop(c, z + s, False).start()

    def cross(c, dx):
        xsend, got = parts[c][:2]
        return pltpu.make_async_remote_copy(
            src_ref=xsend.at[dx - 1],
            dst_ref=got.at[dx],
            send_sem=x_send.at[c, dx - 1],
            recv_sem=x_recv.at[c, dx - 1],
            device_id=row_mate(dx),
            device_id_type=MESH,
        )

    def send_x(c):
        xsend, got = parts[c][:2]
        for dx in (2, 1, 3):
            for k in range(nb):
                xsend[dx - 1, k] = gath[c][tab[dx * nb + k]]
            cross(c, dx).start()
        for k in range(nb):
            got[0, k] = gath[c][tab[k]]

    def share(c, dx, owner):
        view = gath[c].at[pl.ds(owner * nb, nb)]
        return pltpu.make_async_remote_copy(
            src_ref=view,
            dst_ref=view,
            send_sem=x_send.at[c, dx - 1],
            recv_sem=x_recv.at[c, dx - 1],
            device_id=row_mate(dx),
            device_id_type=MESH,
        )

    def climb(c, t, up, last):
        out, inn, fin = parts[c][0 if up else 1], parts[c][2 if up else 3], parts[c][4]
        return pltpu.make_async_remote_copy(
            src_ref=out.at[t],
            dst_ref=fin.at[1 if up else 2] if last else inn.at[t],
            send_sem=(up_send if up else dn_send).at[c, t],
            recv_sem=(up_recv if up else dn_recv).at[c, t],
            device_id=at(site, blk + NX if up else blk - NX),
            device_id_type=MESH,
        )

    def flow(c, j, up):
        out, inn = parts[c][0 if up else 1], parts[c][2 if up else 3]
        first = j == (0 if up else NZ - 1)
        for t in range(NZ - 1, j, -1) if up else range(j):
            if not first:
                climb(c, t, up, False).wait_recv()
            for k in range(nb):
                mine = gath[c][tab[base + t * nb + k]]
                if not first:
                    mine = lax.select(tab[base + (NZ + t) * nb + k] == j, mine, inn[t, k])
                out[t, k] = mine
            climb(c, t, up, abs(t - j) == 1).start()

    def row_stage(c, stage):
        if stage == 0:
            for dx in (2, 1, 3):
                share(c, dx, x).start()
            return
        if stage == 1:
            for dx in (2, 1, 3):
                share(c, dx, (x + NX - dx) % NX).wait_recv()
        j = stage - 1
        if j < NZ - 1:

            @pl.when(z == j)
            def _():
                flow(c, j, True)

            @pl.when(z == NZ - 1 - j)
            def _():
                flow(c, NZ - 1 - j, False)

    def row_end(c):
        fin = parts[c][4]
        for k in range(nb):
            fin[0, k] = gath[c][tab[base + z * nb + k]]

        @pl.when(z > 0)
        def _():
            climb(c, z, True, True).wait_recv()

        @pl.when(z < NZ - 1)
        def _():
            climb(c, z, False, True).wait_recv()

    def picked(c, k):
        if along_z[c]:
            return parts[c][1][tab[NX * nb + k], k]
        source = tab[base + (NZ + z) * nb + k]
        which = jnp.where(source == z, 0, jnp.where(source < z, 1, 2))
        return parts[c][4][which, k]

    state = {}

    def finish(c):
        zfirst, h, blocks = CHUNKS[c]
        if zfirst:
            for dx in (2, 1, 3):
                cross(c, dx).wait_recv()
        else:
            row_end(c)
        if "scale" not in state:
            best = peak_mid[...]
            for d, copy in enumerate(peaks_z):
                copy.wait_recv()
                best = jnp.maximum(best, peak_z[d])
            state["scale"] = best[:1] + EPS
        scale = state["scale"]
        held = {b: [] for b in blocks}
        for k in range(nb):
            value = picked(c, k).astype(jnp.float32) / scale
            for i, b in enumerate(blocks):
                block = value[i * rows : (i + 1) * rows]
                if b == 0:
                    outc_ref[0, k, pl.ds(h * rows, rows)] = block.astype(jnp.bfloat16)
                else:
                    outb_ref[b - 1, 0, k, pl.ds(h * rows, rows)] = block.astype(jnp.bfloat16)
                    held[b].append(block.reshape(rows // 8, 8, m))
        per = rows // 8
        for b in blocks:
            if b == 0:
                continue
            for j in range(nb // 2):
                pair = jnp.concatenate([held[b][2 * j], held[b][2 * j + 1]], axis=1).astype(jnp.bfloat16)
                for f in range(2):
                    lo, hi = max(h * per, f * n_near), min((h + 1) * per, (f + 1) * n_near)
                    if lo < hi:
                        msend[f, pl.ds(lo - f * n_near, hi - lo), b - 1, j] = pair[lo - h * per : hi - h * per]

    def spread(k):
        return pltpu.make_async_remote_copy(
            src_ref=msend.at[:, (near + k) % n_near],
            dst_ref=mrecv.at[k - 1],
            send_sem=m_send.at[k - 1],
            recv_sem=m_recv.at[k - 1],
            device_id=mate(k),
            device_id_type=MESH,
        )

    over = pltpu.make_async_remote_copy(
        src_ref=mpart,
        dst_ref=mcross,
        send_sem=c_send,
        recv_sem=c_recv,
        device_id=across,
        device_id_type=MESH,
    )

    def near_sum():
        for k in range(1, n_near):
            spread(k).wait_recv()

        def total(f):
            value = msend[f, near].astype(jnp.float32)
            for k in range(1, n_near):
                value = value + mrecv[k - 1, f].astype(jnp.float32)
            return value

        mpart[...] = total(1 - far).astype(jnp.bfloat16)
        over.start()
        for c in range(2):
            kept = total(far)[c]
            for j in range(nb // 2):
                sum_ref[c, 2 * j] = kept[j, :8]
                sum_ref[c, 2 * j + 1] = kept[j, 8:]

    def far_sum():
        over.wait_recv()
        for c in range(2):
            for j in range(nb // 2):
                other = mcross[c, j].astype(jnp.float32)
                sum_ref[c, 2 * j] += other[:8]
                sum_ref[c, 2 * j + 1] += other[8:]

    last_b = max(c for c in range(nc) if CHUNKS[c][2] != (0,))
    top = join(0, jnp.float32(0.0))
    for step in range(nc + NZ):
        if step == 1:
            top = join(1, top)
            peak_src[...] = jnp.full(peak_src.shape, top, jnp.float32)
            for copy in peaks_x:
                copy.start()
        for c in range(nc):
            stage = step - c
            if 0 <= stage < NZ:
                if along_z[c]:
                    relay(c, stage)
                    if stage == NZ - 1:
                        send_x(c)
                else:
                    row_stage(c, stage)
            elif stage == NZ:
                if c == nc - 1:
                    near_sum()
                finish(c)
                if c == last_b:
                    for k in (4, 3, 5, 2, 6, 1, 7):
                        spread(k).start()
        if step == 2:
            best = peak_src[...]
            for d, copy in enumerate(peaks_x):
                copy.wait_recv()
                best = jnp.maximum(best, peak_x[d])
            peak_mid[...] = best
            for copy in peaks_z:
                copy.start()
    far_sum()

    for h in range(HALVES):
        for copy in shift(h):
            copy.wait_send()
    for copy in peaks_x + peaks_z:
        copy.wait_send()
    for c in range(nc):
        if not along_z[c]:
            for dx in (1, 2, 3):
                share(c, dx, x).wait_send()
            for t in range(NZ):

                @pl.when(z < t)
                def _():
                    climb(c, t, True, False).wait_send()

                @pl.when(z > t)
                def _():
                    climb(c, t, False, False).wait_send()

            continue
        for s in range(NZ - 1):

            @pl.when(jnp.logical_and(z - s >= 0, z < NZ - 1))
            def _():
                hop(c, z - s, True).wait_send()

            @pl.when(jnp.logical_and(z + s <= NZ - 1, z > 0))
            def _():
                hop(c, z + s, False).wait_send()

        for dx in (1, 2, 3):
            cross(c, dx).wait_send()
    for k in range(1, n_near):
        spread(k).wait_send()
    over.wait_send()


def per_device(n_site, corner, bcorner, edge, bedge, proj, joining, momentum):
    _, nb, m, kdim = edge.shape
    rows = m // HALVES
    nc = len(CHUNKS)
    tall = [rows * len(blocks) for _, _, blocks in CHUNKS]
    n_near = n_site // 2
    bf = jnp.bfloat16
    hbm = pl.BlockSpec(memory_space=pl.ANY)
    smem = pl.BlockSpec(memory_space=pltpu.SMEM)
    vmem = pl.BlockSpec(memory_space=pltpu.VMEM)
    dma = pltpu.SemaphoreType.DMA
    return pl.pallas_call(
        functools.partial(mega, n_site),
        out_shape=(
            jax.ShapeDtypeStruct(corner.shape, bf),
            jax.ShapeDtypeStruct(bcorner.shape, bf),
            jax.ShapeDtypeStruct((2, nb, m // n_site, m), jnp.float32),
        ),
        in_specs=[hbm, smem, hbm, hbm, hbm, hbm, hbm],
        out_specs=(vmem, vmem, vmem),
        scratch_shapes=[
            pltpu.VMEM((nb, m, kdim), bf),
            pltpu.VMEM((nb, m, kdim), bf),
            pltpu.VMEM((nb, kdim, m), bf),
            pltpu.VMEM((HALVES, 3, nb, rows, m), bf),
            pltpu.VMEM((nb, m, m), bf),
            pltpu.VMEM((nb, m, m), bf),
            pltpu.VMEM((8, m), jnp.float32),
            pltpu.VMEM((NX - 1, 8, m), jnp.float32),
            pltpu.VMEM((8, m), jnp.float32),
            pltpu.VMEM((NZ - 1, 8, m), jnp.float32),
            pltpu.VMEM((2, n_near, 2, nb // 2, 16, m), bf),
            pltpu.VMEM((n_near - 1, 2, 2, nb // 2, 16, m), bf),
            pltpu.VMEM((2, nb // 2, 16, m), bf),
            pltpu.VMEM((2, nb // 2, 16, m), bf),
            pltpu.SMEM(((NX + 1 + 2 * NZ) * nb,), jnp.int32),
            pltpu.SMEM(joining.shape, jnp.int32),
        ]
        + [pltpu.VMEM((NZ * nb, t, m), bf) for t in tall]
        + [pltpu.VMEM((NZ, nb, t, m), bf) for t in tall for _ in range(5)]
        + [
            dma((3, nb)),
            dma((HALVES, 3)),
            dma((HALVES, 3)),
            dma((nc, NZ - 1)),
            dma((nc, NZ - 1)),
            dma((nc, NZ)),
            dma((nc, NX - 1)),
            dma((nc, NX - 1)),
            dma((nc, NZ)),
            dma((nc, NZ)),
            dma((nc, NZ)),
            dma((nc, NZ)),
            dma((2, NX - 1)),
            dma((2, NX - 1)),
            dma((n_near - 1,)),
            dma((n_near - 1,)),
            dma,
            dma,
            dma,
        ],
        compiler_params=pltpu.CompilerParams(
            collective_id=0, has_side_effects=True, vmem_limit_bytes=62 << 20
        ),
        name="column_move",
    )(joining, momentum, corner, bcorner, edge, bedge, proj)


def solution(mesh):
    in_specs = (
        P("site", "blk", None, None),
        P(None, "site", "blk", None, None),
        P("site", "blk", None, None),
        P("site", "blk", None, None),
        P("site", "blk", None, None),
        P("site", None),
        P(),
    )
    out_specs = (
        P("site", "blk", None, None),
        P(None, "site", "blk", None, None),
        P(None, "blk", "site", None),
    )
    return jax.shard_map(
        functools.partial(per_device, mesh.shape["site"]),
        mesh=mesh,
        in_specs=in_specs,
        out_specs=out_specs,
        check_vma=False,
    )
```

```python
import functools

import jax
import jax.numpy as jnp
from jax import lax
from jax.experimental import pallas as pl
from jax.experimental.pallas import tpu as pltpu
from jax.sharding import PartitionSpec as P

EPS = 1e-6
MESH = pl.DeviceIdType.MESH
NX = 4
NZ = 4
HALVES = 2
CHUNKS = (
    (True, 0, (1,), 0),
    (False, 0, (2,), 0),
    (True, 0, (0,), 1),
    (False, 1, (1,), 1),
    (True, 1, (2,), 1),
    (False, 1, (0,), 2),
)


def mega(
    n_site,
    join_ref,
    mom_ref,
    corner_ref,
    bcorner_ref,
    edge_ref,
    bedge_ref,
    proj_ref,
    outc_ref,
    outb_ref,
    sum_ref,
    edge_v,
    bedge_v,
    proj_v,
    cb_v,
    e_v,
    d_v,
    peak_src,
    peak_x,
    peak_mid,
    peak_z,
    msend,
    mrecv,
    mpart,
    mcross,
    tab,
    jsm,
    *rest,
):
    nb = edge_v.shape[0]
    m = cb_v.shape[-1]
    rows = m // HALVES
    nc = len(CHUNKS)
    along_z = [chunk[0] for chunk in CHUNKS]
    n_near = n_site // 2
    gath = rest[:nc]
    parts = [rest[nc + 5 * i : nc + 5 * i + 5] for i in range(nc)]
    (load_sem, s_send, s_recv, z_up, z_down, z_recv, x_send, x_recv, up_send, up_recv, dn_send, dn_recv, p_send, p_recv, m_send, m_recv, c_send, c_recv, j_sem) = rest[
        6 * nc :
    ]

    site = lax.axis_index("site")
    blk = lax.axis_index("blk")
    z = blk // NX
    x = blk % NX

    def at(s, b):
        return {"site": s, "blk": b}

    barrier = pltpu.get_barrier_semaphore()
    near, far = site % n_near, site // n_near

    def mate(k):
        return at(far * n_near + (near + k) % n_near, blk)

    def row_mate(dx):
        return at(site, z * NX + (x + dx) % NX)

    def column_mate(dz):
        return at(site, (z + dz) % NZ * NX + x)

    right, left = at((site + 1) % n_site, blk), at((site + n_site - 1) % n_site, blk)
    across = at((site + n_near) % n_site, blk)
    partners = (
        [right, left, across]
        + [mate(k) for k in range(1, n_near)]
        + [row_mate(d) for d in range(1, NX)]
        + [column_mate(d) for d in range(1, NZ)]
    )
    for partner in partners:
        pl.semaphore_signal(barrier, inc=1, device_id=partner, device_id_type=MESH)

    def loads(q):
        return [
            pltpu.make_async_copy(src.at[0, q], dst.at[q], load_sem.at[i, q])
            for i, (src, dst) in enumerate(((edge_ref, edge_v), (bedge_ref, bedge_v), (proj_ref, proj_v)))
        ]

    fetch = pltpu.make_async_copy(join_ref, jsm, j_sem)
    fetch.start()
    for q in range(nb):
        for copy in loads(q):
            copy.start()

    base = (NX + 1) * nb
    fetch.wait()
    for dx in range(NX):
        target = z * NX + (x + dx) % NX
        for k in range(nb):
            src = jsm[0, target * nb + k]
            dev = src // nb
            tab[dx * nb + k] = (dev // NX) * nb + (src - dev * nb)
            if dx == 0:
                tab[NX * nb + k] = (x - dev % NX + NX) % NX
    for t in range(NZ):
        for k in range(nb):
            src = jsm[0, (t * NX + x) * nb + k]
            dev = src // nb
            tab[base + t * nb + k] = (dev % NX) * nb + (src - dev * nb)
            tab[base + (NZ + t) * nb + k] = dev // NX

    pl.semaphore_wait(barrier, len(partners))

    def shift(h):
        part = pl.ds(h * rows, rows)
        sources = [corner_ref.at[0, :, part]] + [bcorner_ref.at[c, 0, :, part] for c in range(2)]
        return [
            pltpu.make_async_remote_copy(
                src_ref=source,
                dst_ref=cb_v.at[h, c],
                send_sem=s_send.at[h, c],
                recv_sem=s_recv.at[h, c],
                device_id=right,
                device_id_type=MESH,
            )
            for c, source in enumerate(sources)
        ]

    for h in range(HALVES):
        for copy in shift(h):
            copy.start()

    def local(q, carry):
        for copy in loads(q):
            copy.wait()
        both = jnp.concatenate([edge_v[q], bedge_v[q]], axis=0)
        prod = jnp.dot(both, proj_v[q], preferred_element_type=jnp.float32).astype(jnp.bfloat16)
        e_v[q] = prod[:m]
        d_v[q] = prod[m:]
        return carry

    lax.fori_loop(0, nb, local, 0)

    angle = jnp.full((8, m), mom_ref[0] * site.astype(jnp.float32), jnp.float32)
    cosine = jnp.cos(angle)[:1]
    sine = jnp.sin(angle)[:1]

    def join(h, top):
        for copy in shift(h):
            copy.wait_recv()

        def join_slot(q, top):
            left_rows = jnp.concatenate([cb_v[h, 0, q], cb_v[h, 1, q], cb_v[h, 2, q]], axis=0)
            main = jnp.dot(left_rows, e_v[q], preferred_element_type=jnp.float32)
            inserted = jnp.dot(cb_v[h, 0, q], d_v[q], preferred_element_type=jnp.float32)
            real, imag = main[rows : 2 * rows], main[2 * rows :]
            blocks = [
                main[:rows].astype(jnp.bfloat16),
                (cosine * real - sine * imag + inserted).astype(jnp.bfloat16),
                (sine * real + cosine * imag).astype(jnp.bfloat16),
            ]
            for c, (zfirst, half, held, _) in enumerate(CHUNKS):
                if half == h:
                    for i, b in enumerate(held):
                        gath[c][(z if zfirst else x) * nb + q, pl.ds(i * rows, rows)] = blocks[b]
            return jnp.maximum(top, jnp.max(jnp.abs(blocks[0].astype(jnp.float32))))

        return lax.fori_loop(0, nb, join_slot, top)

    peaks_x = [
        pltpu.make_async_remote_copy(
            src_ref=peak_src,
            dst_ref=peak_x.at[d - 1],
            send_sem=p_send.at[0, d - 1],
            recv_sem=p_recv.at[0, d - 1],
            device_id=row_mate(d),
            device_id_type=MESH,
        )
        for d in range(1, NX)
    ]
    peaks_z = [
        pltpu.make_async_remote_copy(
            src_ref=peak_mid,
            dst_ref=peak_z.at[d - 1],
            send_sem=p_send.at[1, d - 1],
            recv_sem=p_recv.at[1, d - 1],
            device_id=column_mate(d),
            device_id_type=MESH,
        )
        for d in range(1, NZ)
    ]

    def hop(c, j, up):
        sems = z_up if up else z_down
        step = z - j if up else j - z
        view = gath[c].at[pl.ds(j * nb, nb)]
        return pltpu.make_async_remote_copy(
            src_ref=view,
            dst_ref=view,
            send_sem=sems.at[c, step],
            recv_sem=z_recv.at[c, j],
            device_id=at(site, blk + NX if up else blk - NX),
            device_id_type=MESH,
        )

    def relay(c, s):
        @pl.when(z - s >= 0)
        def _():
            if s > 0:
                hop(c, z - s, True).wait_recv()

            if s < NZ - 1:

                @pl.when(z < NZ - 1)
                def _():
                    hop(c, z - s, True).start()

        @pl.when(z + s <= NZ - 1)
        def _():
            if s > 0:
                hop(c, z + s, False).wait_recv()

            if s < NZ - 1:

                @pl.when(z > 0)
                def _():
                    hop(c, z + s, False).start()

    def cross(c, dx):
        xsend, got = parts[c][:2]
        return pltpu.make_async_remote_copy(
            src_ref=xsend.at[dx - 1],
            dst_ref=got.at[dx],
            send_sem=x_send.at[c, dx - 1],
            recv_sem=x_recv.at[c, dx - 1],
            device_id=row_mate(dx),
            device_id_type=MESH,
        )

    def send_x(c):
        xsend, got = parts[c][:2]
        for dx in (2, 1, 3):
            for k in range(nb):
                xsend[dx - 1, k] = gath[c][tab[dx * nb + k]]
            cross(c, dx).start()
        for k in range(nb):
            got[0, k] = gath[c][tab[k]]

    def share(c, dx, owner):
        view = gath[c].at[pl.ds(owner * nb, nb)]
        return pltpu.make_async_remote_copy(
            src_ref=view,
            dst_ref=view,
            send_sem=x_send.at[c, dx - 1],
            recv_sem=x_recv.at[c, dx - 1],
            device_id=row_mate(dx),
            device_id_type=MESH,
        )

    def climb(c, t, up, last):
        out, inn, fin = parts[c][0 if up else 1], parts[c][2 if up else 3], parts[c][4]
        return pltpu.make_async_remote_copy(
            src_ref=out.at[t],
            dst_ref=fin.at[1 if up else 2] if last else inn.at[t],
            send_sem=(up_send if up else dn_send).at[c, t],
            recv_sem=(up_recv if up else dn_recv).at[c, t],
            device_id=at(site, blk + NX if up else blk - NX),
            device_id_type=MESH,
        )

    def flow(c, j, up):
        out, inn = parts[c][0 if up else 1], parts[c][2 if up else 3]
        first = j == (0 if up else NZ - 1)
        for t in range(NZ - 1, j, -1) if up else range(j):
            if not first:
                climb(c, t, up, False).wait_recv()
            for k in range(nb):
                mine = gath[c][tab[base + t * nb + k]]
                if not first:
                    mine = lax.select(tab[base + (NZ + t) * nb + k] == j, mine, inn[t, k])
                out[t, k] = mine
            climb(c, t, up, abs(t - j) == 1).start()

    def row_stage(c, stage):
        if stage == 0:
            for dx in (2, 1, 3):
                share(c, dx, x).start()
            return
        if stage == 1:
            for dx in (2, 1, 3):
                share(c, dx, (x + NX - dx) % NX).wait_recv()
        j = stage - 1
        if j < NZ - 1:

            @pl.when(z == j)
            def _():
                flow(c, j, True)

            @pl.when(z == NZ - 1 - j)
            def _():
                flow(c, NZ - 1 - j, False)

    def row_end(c):
        fin = parts[c][4]
        for k in range(nb):
            fin[0, k] = gath[c][tab[base + z * nb + k]]

        @pl.when(z > 0)
        def _():
            climb(c, z, True, True).wait_recv()

        @pl.when(z < NZ - 1)
        def _():
            climb(c, z, False, True).wait_recv()

    def picked(c, k):
        if along_z[c]:
            return parts[c][1][tab[NX * nb + k], k]
        source = tab[base + (NZ + z) * nb + k]
        which = jnp.where(source == z, 0, jnp.where(source < z, 1, 2))
        return parts[c][4][which, k]

    state = {}

    def finish(c):
        zfirst, h, blocks, _ = CHUNKS[c]
        if zfirst:
            for dx in (2, 1, 3):
                cross(c, dx).wait_recv()
        else:
            row_end(c)
        if "scale" not in state:
            best = peak_mid[...]
            for d, copy in enumerate(peaks_z):
                copy.wait_recv()
                best = jnp.maximum(best, peak_z[d])
            state["scale"] = best[:1] + EPS
        scale = state["scale"]
        held = {b: [] for b in blocks}
        for k in range(nb):
            value = picked(c, k).astype(jnp.float32) / scale
            for i, b in enumerate(blocks):
                block = value[i * rows : (i + 1) * rows]
                if b == 0:
                    outc_ref[0, k, pl.ds(h * rows, rows)] = block.astype(jnp.bfloat16)
                else:
                    outb_ref[b - 1, 0, k, pl.ds(h * rows, rows)] = block.astype(jnp.bfloat16)
                    held[b].append(block.reshape(rows // 8, 8, m))
        per = rows // 8
        for b in blocks:
            if b == 0:
                continue
            for j in range(nb // 2):
                pair = jnp.concatenate([held[b][2 * j], held[b][2 * j + 1]], axis=1).astype(jnp.bfloat16)
                for f in range(2):
                    lo, hi = max(h * per, f * n_near), min((h + 1) * per, (f + 1) * n_near)
                    if lo < hi:
                        msend[f, pl.ds(lo - f * n_near, hi - lo), b - 1, j] = pair[lo - h * per : hi - h * per]

    def spread(k):
        return pltpu.make_async_remote_copy(
            src_ref=msend.at[:, (near + k) % n_near],
            dst_ref=mrecv.at[k - 1],
            send_sem=m_send.at[k - 1],
            recv_sem=m_recv.at[k - 1],
            device_id=mate(k),
            device_id_type=MESH,
        )

    over = pltpu.make_async_remote_copy(
        src_ref=mpart,
        dst_ref=mcross,
        send_sem=c_send,
        recv_sem=c_recv,
        device_id=across,
        device_id_type=MESH,
    )

    def near_sum():
        for k in range(1, n_near):
            spread(k).wait_recv()

        def total(f):
            value = msend[f, near].astype(jnp.float32)
            for k in range(1, n_near):
                value = value + mrecv[k - 1, f].astype(jnp.float32)
            return value

        mpart[...] = total(1 - far).astype(jnp.bfloat16)
        over.start()
        for c in range(2):
            kept = total(far)[c]
            for j in range(nb // 2):
                sum_ref[c, 2 * j] = kept[j, :8]
                sum_ref[c, 2 * j + 1] = kept[j, 8:]

    def far_sum():
        over.wait_recv()
        for c in range(2):
            for j in range(nb // 2):
                other = mcross[c, j].astype(jnp.float32)
                sum_ref[c, 2 * j] += other[:8]
                sum_ref[c, 2 * j + 1] += other[8:]

    last_b = max(c for c in range(nc) if CHUNKS[c][2] != (0,))
    top = join(0, jnp.float32(0.0))
    for step in range(max(chunk[3] for chunk in CHUNKS) + NZ + 1):
        if step == 1:
            top = join(1, top)
            peak_src[...] = jnp.full(peak_src.shape, top, jnp.float32)
            for copy in peaks_x:
                copy.start()
        for c in range(nc):
            stage = step - CHUNKS[c][3]
            if 0 <= stage < NZ:
                if along_z[c]:
                    relay(c, stage)
                    if stage == NZ - 1:
                        send_x(c)
                else:
                    row_stage(c, stage)
            elif stage == NZ:
                if c == nc - 1:
                    near_sum()
                finish(c)
                if c == last_b:
                    for k in (4, 3, 5, 2, 6, 1, 7):
                        spread(k).start()
        if step == 2:
            best = peak_src[...]
            for d, copy in enumerate(peaks_x):
                copy.wait_recv()
                best = jnp.maximum(best, peak_x[d])
            peak_mid[...] = best
            for copy in peaks_z:
                copy.start()
    far_sum()

    for h in range(HALVES):
        for copy in shift(h):
            copy.wait_send()
    for copy in peaks_x + peaks_z:
        copy.wait_send()
    for c in range(nc):
        if not along_z[c]:
            for dx in (1, 2, 3):
                share(c, dx, x).wait_send()
            for t in range(NZ):

                @pl.when(z < t)
                def _():
                    climb(c, t, True, False).wait_send()

                @pl.when(z > t)
                def _():
                    climb(c, t, False, False).wait_send()

            continue
        for s in range(NZ - 1):

            @pl.when(jnp.logical_and(z - s >= 0, z < NZ - 1))
            def _():
                hop(c, z - s, True).wait_send()

            @pl.when(jnp.logical_and(z + s <= NZ - 1, z > 0))
            def _():
                hop(c, z + s, False).wait_send()

        for dx in (1, 2, 3):
            cross(c, dx).wait_send()
    for k in range(1, n_near):
        spread(k).wait_send()
    over.wait_send()


def per_device(n_site, corner, bcorner, edge, bedge, proj, joining, momentum):
    _, nb, m, kdim = edge.shape
    rows = m // HALVES
    nc = len(CHUNKS)
    tall = [rows * len(chunk[2]) for chunk in CHUNKS]
    n_near = n_site // 2
    bf = jnp.bfloat16
    hbm = pl.BlockSpec(memory_space=pl.ANY)
    smem = pl.BlockSpec(memory_space=pltpu.SMEM)
    vmem = pl.BlockSpec(memory_space=pltpu.VMEM)
    dma = pltpu.SemaphoreType.DMA
    return pl.pallas_call(
        functools.partial(mega, n_site),
        out_shape=(
            jax.ShapeDtypeStruct(corner.shape, bf),
            jax.ShapeDtypeStruct(bcorner.shape, bf),
            jax.ShapeDtypeStruct((2, nb, m // n_site, m), jnp.float32),
        ),
        in_specs=[hbm, smem, hbm, hbm, hbm, hbm, hbm],
        out_specs=(vmem, vmem, vmem),
        scratch_shapes=[
            pltpu.VMEM((nb, m, kdim), bf),
            pltpu.VMEM((nb, m, kdim), bf),
            pltpu.VMEM((nb, kdim, m), bf),
            pltpu.VMEM((HALVES, 3, nb, rows, m), bf),
            pltpu.VMEM((nb, m, m), bf),
            pltpu.VMEM((nb, m, m), bf),
            pltpu.VMEM((8, m), jnp.float32),
            pltpu.VMEM((NX - 1, 8, m), jnp.float32),
            pltpu.VMEM((8, m), jnp.float32),
            pltpu.VMEM((NZ - 1, 8, m), jnp.float32),
            pltpu.VMEM((2, n_near, 2, nb // 2, 16, m), bf),
            pltpu.VMEM((n_near - 1, 2, 2, nb // 2, 16, m), bf),
            pltpu.VMEM((2, nb // 2, 16, m), bf),
            pltpu.VMEM((2, nb // 2, 16, m), bf),
            pltpu.SMEM(((NX + 1 + 2 * NZ) * nb,), jnp.int32),
            pltpu.SMEM(joining.shape, jnp.int32),
        ]
        + [pltpu.VMEM((NZ * nb, t, m), bf) for t in tall]
        + [pltpu.VMEM((NZ, nb, t, m), bf) for t in tall for _ in range(5)]
        + [
            dma((3, nb)),
            dma((HALVES, 3)),
            dma((HALVES, 3)),
            dma((nc, NZ - 1)),
            dma((nc, NZ - 1)),
            dma((nc, NZ)),
            dma((nc, NX - 1)),
            dma((nc, NX - 1)),
            dma((nc, NZ)),
            dma((nc, NZ)),
            dma((nc, NZ)),
            dma((nc, NZ)),
            dma((2, NX - 1)),
            dma((2, NX - 1)),
            dma((n_near - 1,)),
            dma((n_near - 1,)),
            dma,
            dma,
            dma,
        ],
        compiler_params=pltpu.CompilerParams(
            collective_id=0, has_side_effects=True, vmem_limit_bytes=62 << 20
        ),
        name="column_move",
    )(joining, momentum, corner, bcorner, edge, bedge, proj)


def solution(mesh):
    in_specs = (
        P("site", "blk", None, None),
        P(None, "site", "blk", None, None),
        P("site", "blk", None, None),
        P("site", "blk", None, None),
        P("site", "blk", None, None),
        P("site", None),
        P(),
    )
    out_specs = (
        P("site", "blk", None, None),
        P(None, "site", "blk", None, None),
        P(None, "blk", "site", None),
    )
    return jax.shard_map(
        functools.partial(per_device, mesh.shape["site"]),
        mesh=mesh,
        in_specs=in_specs,
        out_specs=out_specs,
        check_vma=False,
    )
```

```python
import functools

import jax
import jax.numpy as jnp
from jax import lax
from jax.experimental import pallas as pl
from jax.experimental.pallas import tpu as pltpu
from jax.sharding import PartitionSpec as P

EPS = 1e-6
MESH = pl.DeviceIdType.MESH
NX = 4
NZ = 4
HALVES = 2
CHUNKS = (
    (True, 0, (1,), 0),
    (False, 0, (2,), 0),
    (False, 1, (1,), 1),
    (True, 1, (2,), 1),
    (True, 0, (0,), 1),
    (False, 1, (0,), 2),
)


def mega(
    n_site,
    join_ref,
    mom_ref,
    corner_ref,
    bcorner_ref,
    edge_ref,
    bedge_ref,
    proj_ref,
    outc_ref,
    outb_ref,
    sum_ref,
    edge_v,
    bedge_v,
    proj_v,
    cb_v,
    e_v,
    d_v,
    peak_src,
    peak_x,
    peak_mid,
    peak_z,
    msend,
    mrecv,
    mpart,
    mcross,
    tab,
    jsm,
    *rest,
):
    nb = edge_v.shape[0]
    m = cb_v.shape[-1]
    rows = m // HALVES
    nc = len(CHUNKS)
    along_z = [chunk[0] for chunk in CHUNKS]
    n_near = n_site // 2
    gath = rest[:nc]
    parts = [rest[nc + 5 * i : nc + 5 * i + 5] for i in range(nc)]
    (load_sem, s_send, s_recv, z_up, z_down, z_recv, x_send, x_recv, up_send, up_recv, dn_send, dn_recv, p_send, p_recv, m_send, m_recv, c_send, c_recv, j_sem) = rest[
        6 * nc :
    ]

    site = lax.axis_index("site")
    blk = lax.axis_index("blk")
    z = blk // NX
    x = blk % NX

    def at(s, b):
        return {"site": s, "blk": b}

    barrier = pltpu.get_barrier_semaphore()
    near, far = site % n_near, site // n_near

    def mate(k):
        return at(far * n_near + (near + k) % n_near, blk)

    def row_mate(dx):
        return at(site, z * NX + (x + dx) % NX)

    def column_mate(dz):
        return at(site, (z + dz) % NZ * NX + x)

    right, left = at((site + 1) % n_site, blk), at((site + n_site - 1) % n_site, blk)
    across = at((site + n_near) % n_site, blk)
    partners = (
        [right, left, across]
        + [mate(k) for k in range(1, n_near)]
        + [row_mate(d) for d in range(1, NX)]
        + [column_mate(d) for d in range(1, NZ)]
    )
    for partner in partners:
        pl.semaphore_signal(barrier, inc=1, device_id=partner, device_id_type=MESH)

    def loads(q):
        return [
            pltpu.make_async_copy(src.at[0, q], dst.at[q], load_sem.at[i, q])
            for i, (src, dst) in enumerate(((edge_ref, edge_v), (bedge_ref, bedge_v), (proj_ref, proj_v)))
        ]

    fetch = pltpu.make_async_copy(join_ref, jsm, j_sem)
    fetch.start()
    for q in range(nb):
        for copy in loads(q):
            copy.start()

    base = (NX + 1) * nb
    fetch.wait()
    for dx in range(NX):
        target = z * NX + (x + dx) % NX
        for k in range(nb):
            src = jsm[0, target * nb + k]
            dev = src // nb
            tab[dx * nb + k] = (dev // NX) * nb + (src - dev * nb)
            if dx == 0:
                tab[NX * nb + k] = (x - dev % NX + NX) % NX
    for t in range(NZ):
        for k in range(nb):
            src = jsm[0, (t * NX + x) * nb + k]
            dev = src // nb
            tab[base + t * nb + k] = (dev % NX) * nb + (src - dev * nb)
            tab[base + (NZ + t) * nb + k] = dev // NX

    pl.semaphore_wait(barrier, len(partners))

    def shift(h):
        part = pl.ds(h * rows, rows)
        sources = [corner_ref.at[0, :, part]] + [bcorner_ref.at[c, 0, :, part] for c in range(2)]
        return [
            pltpu.make_async_remote_copy(
                src_ref=source,
                dst_ref=cb_v.at[h, c],
                send_sem=s_send.at[h, c],
                recv_sem=s_recv.at[h, c],
                device_id=right,
                device_id_type=MESH,
            )
            for c, source in enumerate(sources)
        ]

    for h in range(HALVES):
        for copy in shift(h):
            copy.start()

    def local(q, carry):
        for copy in loads(q):
            copy.wait()
        both = jnp.concatenate([edge_v[q], bedge_v[q]], axis=0)
        prod = jnp.dot(both, proj_v[q], preferred_element_type=jnp.float32).astype(jnp.bfloat16)
        e_v[q] = prod[:m]
        d_v[q] = prod[m:]
        return carry

    lax.fori_loop(0, nb, local, 0)

    angle = jnp.full((8, m), mom_ref[0] * site.astype(jnp.float32), jnp.float32)
    cosine = jnp.cos(angle)[:1]
    sine = jnp.sin(angle)[:1]

    def join(h, top):
        for copy in shift(h):
            copy.wait_recv()

        def join_slot(q, top):
            left_rows = jnp.concatenate([cb_v[h, 0, q], cb_v[h, 1, q], cb_v[h, 2, q]], axis=0)
            main = jnp.dot(left_rows, e_v[q], preferred_element_type=jnp.float32)
            inserted = jnp.dot(cb_v[h, 0, q], d_v[q], preferred_element_type=jnp.float32)
            real, imag = main[rows : 2 * rows], main[2 * rows :]
            blocks = [
                main[:rows].astype(jnp.bfloat16),
                (cosine * real - sine * imag + inserted).astype(jnp.bfloat16),
                (sine * real + cosine * imag).astype(jnp.bfloat16),
            ]
            for c, (zfirst, half, held, _) in enumerate(CHUNKS):
                if half == h:
                    for i, b in enumerate(held):
                        gath[c][(z if zfirst else x) * nb + q, pl.ds(i * rows, rows)] = blocks[b]
            return jnp.maximum(top, jnp.max(jnp.abs(blocks[0].astype(jnp.float32))))

        return lax.fori_loop(0, nb, join_slot, top)

    peaks_x = [
        pltpu.make_async_remote_copy(
            src_ref=peak_src,
            dst_ref=peak_x.at[d - 1],
            send_sem=p_send.at[0, d - 1],
            recv_sem=p_recv.at[0, d - 1],
            device_id=row_mate(d),
            device_id_type=MESH,
        )
        for d in range(1, NX)
    ]
    peaks_z = [
        pltpu.make_async_remote_copy(
            src_ref=peak_mid,
            dst_ref=peak_z.at[d - 1],
            send_sem=p_send.at[1, d - 1],
            recv_sem=p_recv.at[1, d - 1],
            device_id=column_mate(d),
            device_id_type=MESH,
        )
        for d in range(1, NZ)
    ]

    def hop(c, j, up):
        sems = z_up if up else z_down
        step = z - j if up else j - z
        view = gath[c].at[pl.ds(j * nb, nb)]
        return pltpu.make_async_remote_copy(
            src_ref=view,
            dst_ref=view,
            send_sem=sems.at[c, step],
            recv_sem=z_recv.at[c, j],
            device_id=at(site, blk + NX if up else blk - NX),
            device_id_type=MESH,
        )

    def relay(c, s):
        @pl.when(z - s >= 0)
        def _():
            if s > 0:
                hop(c, z - s, True).wait_recv()

            if s < NZ - 1:

                @pl.when(z < NZ - 1)
                def _():
                    hop(c, z - s, True).start()

        @pl.when(z + s <= NZ - 1)
        def _():
            if s > 0:
                hop(c, z + s, False).wait_recv()

            if s < NZ - 1:

                @pl.when(z > 0)
                def _():
                    hop(c, z + s, False).start()

    def cross(c, dx):
        xsend, got = parts[c][:2]
        return pltpu.make_async_remote_copy(
            src_ref=xsend.at[dx - 1],
            dst_ref=got.at[dx],
            send_sem=x_send.at[c, dx - 1],
            recv_sem=x_recv.at[c, dx - 1],
            device_id=row_mate(dx),
            device_id_type=MESH,
        )

    def send_x(c):
        xsend, got = parts[c][:2]
        for dx in (2, 1, 3):
            for k in range(nb):
                xsend[dx - 1, k] = gath[c][tab[dx * nb + k]]
            cross(c, dx).start()
        for k in range(nb):
            got[0, k] = gath[c][tab[k]]

    def share(c, dx, owner):
        view = gath[c].at[pl.ds(owner * nb, nb)]
        return pltpu.make_async_remote_copy(
            src_ref=view,
            dst_ref=view,
            send_sem=x_send.at[c, dx - 1],
            recv_sem=x_recv.at[c, dx - 1],
            device_id=row_mate(dx),
            device_id_type=MESH,
        )

    def climb(c, t, up, last):
        out, inn, fin = parts[c][0 if up else 1], parts[c][2 if up else 3], parts[c][4]
        return pltpu.make_async_remote_copy(
            src_ref=out.at[t],
            dst_ref=fin.at[1 if up else 2] if last else inn.at[t],
            send_sem=(up_send if up else dn_send).at[c, t],
            recv_sem=(up_recv if up else dn_recv).at[c, t],
            device_id=at(site, blk + NX if up else blk - NX),
            device_id_type=MESH,
        )

    def flow(c, j, up):
        out, inn = parts[c][0 if up else 1], parts[c][2 if up else 3]
        first = j == (0 if up else NZ - 1)
        for t in range(NZ - 1, j, -1) if up else range(j):
            if not first:
                climb(c, t, up, False).wait_recv()
            for k in range(nb):
                mine = gath[c][tab[base + t * nb + k]]
                if not first:
                    mine = lax.select(tab[base + (NZ + t) * nb + k] == j, mine, inn[t, k])
                out[t, k] = mine
            climb(c, t, up, abs(t - j) == 1).start()

    def row_stage(c, stage):
        if stage == 0:
            for dx in (2, 1, 3):
                share(c, dx, x).start()
            return
        if stage == 1:
            for dx in (2, 1, 3):
                share(c, dx, (x + NX - dx) % NX).wait_recv()
        j = stage - 1
        if j < NZ - 1:

            @pl.when(z == j)
            def _():
                flow(c, j, True)

            @pl.when(z == NZ - 1 - j)
            def _():
                flow(c, NZ - 1 - j, False)

    def row_end(c):
        fin = parts[c][4]
        for k in range(nb):
            fin[0, k] = gath[c][tab[base + z * nb + k]]

        @pl.when(z > 0)
        def _():
            climb(c, z, True, True).wait_recv()

        @pl.when(z < NZ - 1)
        def _():
            climb(c, z, False, True).wait_recv()

    def picked(c, k):
        if along_z[c]:
            return parts[c][1][tab[NX * nb + k], k]
        source = tab[base + (NZ + z) * nb + k]
        which = jnp.where(source == z, 0, jnp.where(source < z, 1, 2))
        return parts[c][4][which, k]

    state = {}

    def finish(c):
        zfirst, h, blocks, _ = CHUNKS[c]
        if zfirst:
            for dx in (2, 1, 3):
                cross(c, dx).wait_recv()
        else:
            row_end(c)
        if "scale" not in state:
            best = peak_mid[...]
            for d, copy in enumerate(peaks_z):
                copy.wait_recv()
                best = jnp.maximum(best, peak_z[d])
            state["scale"] = best[:1] + EPS
        scale = state["scale"]
        held = {b: [] for b in blocks}
        for k in range(nb):
            value = picked(c, k).astype(jnp.float32) / scale
            for i, b in enumerate(blocks):
                block = value[i * rows : (i + 1) * rows]
                if b == 0:
                    outc_ref[0, k, pl.ds(h * rows, rows)] = block.astype(jnp.bfloat16)
                else:
                    outb_ref[b - 1, 0, k, pl.ds(h * rows, rows)] = block.astype(jnp.bfloat16)
                    held[b].append(block.reshape(rows // 8, 8, m))
        per = rows // 8
        for b in blocks:
            if b == 0:
                continue
            for j in range(nb // 2):
                pair = jnp.concatenate([held[b][2 * j], held[b][2 * j + 1]], axis=1).astype(jnp.bfloat16)
                for f in range(2):
                    lo, hi = max(h * per, f * n_near), min((h + 1) * per, (f + 1) * n_near)
                    if lo < hi:
                        msend[f, pl.ds(lo - f * n_near, hi - lo), b - 1, j] = pair[lo - h * per : hi - h * per]

    def spread(f, k):
        return pltpu.make_async_remote_copy(
            src_ref=msend.at[f, (near + k) % n_near],
            dst_ref=mrecv.at[f, k - 1],
            send_sem=m_send.at[f, k - 1],
            recv_sem=m_recv.at[f, k - 1],
            device_id=mate(k),
            device_id_type=MESH,
        )

    over = pltpu.make_async_remote_copy(
        src_ref=mpart,
        dst_ref=mcross,
        send_sem=c_send,
        recv_sem=c_recv,
        device_id=across,
        device_id_type=MESH,
    )

    def near_sum(f):
        total = msend[f, near].astype(jnp.float32)
        for k in range(1, n_near):
            spread(f, k).wait_recv()
            total = total + mrecv[f, k - 1].astype(jnp.float32)

        @pl.when(far == f)
        def _():
            for c in range(2):
                for j in range(nb // 2):
                    sum_ref[c, 2 * j] = total[c, j, :8]
                    sum_ref[c, 2 * j + 1] = total[c, j, 8:]

        @pl.when(far != f)
        def _():
            mpart[...] = total.astype(jnp.bfloat16)
            over.start()

    def far_sum():
        over.wait_recv()
        for c in range(2):
            for j in range(nb // 2):
                other = mcross[c, j].astype(jnp.float32)
                sum_ref[c, 2 * j] += other[:8]
                sum_ref[c, 2 * j + 1] += other[8:]

    last_b = [max(c for c in range(nc) if CHUNKS[c][1] == h and CHUNKS[c][2] != (0,)) for h in range(HALVES)]
    top = join(0, jnp.float32(0.0))
    for step in range(max(chunk[3] for chunk in CHUNKS) + NZ + 1):
        if step == 1:
            top = join(1, top)
            peak_src[...] = jnp.full(peak_src.shape, top, jnp.float32)
            for copy in peaks_x:
                copy.start()
        for c in range(nc):
            stage = step - CHUNKS[c][3]
            if 0 <= stage < NZ:
                if along_z[c]:
                    relay(c, stage)
                    if stage == NZ - 1:
                        send_x(c)
                else:
                    row_stage(c, stage)
        for c in range(nc):
            stage = step - CHUNKS[c][3]
            if stage == NZ:
                if c == nc - 1:
                    near_sum(1)
                finish(c)
                for f in range(HALVES):
                    if c == last_b[f]:
                        for k in (4, 3, 5, 2, 6, 1, 7):
                            spread(f, k).start()
                if c == last_b[1]:
                    near_sum(0)
        if step == 2:
            best = peak_src[...]
            for d, copy in enumerate(peaks_x):
                copy.wait_recv()
                best = jnp.maximum(best, peak_x[d])
            peak_mid[...] = best
            for copy in peaks_z:
                copy.start()
    far_sum()

    for h in range(HALVES):
        for copy in shift(h):
            copy.wait_send()
    for copy in peaks_x + peaks_z:
        copy.wait_send()
    for c in range(nc):
        if not along_z[c]:
            for dx in (1, 2, 3):
                share(c, dx, x).wait_send()
            for t in range(NZ):

                @pl.when(z < t)
                def _():
                    climb(c, t, True, False).wait_send()

                @pl.when(z > t)
                def _():
                    climb(c, t, False, False).wait_send()

            continue
        for s in range(NZ - 1):

            @pl.when(jnp.logical_and(z - s >= 0, z < NZ - 1))
            def _():
                hop(c, z - s, True).wait_send()

            @pl.when(jnp.logical_and(z + s <= NZ - 1, z > 0))
            def _():
                hop(c, z + s, False).wait_send()

        for dx in (1, 2, 3):
            cross(c, dx).wait_send()
    for f in range(HALVES):
        for k in range(1, n_near):
            spread(f, k).wait_send()
    over.wait_send()


def store(*refs):
    n = (len(refs) - 1) // 2
    copies = [pltpu.make_async_copy(refs[i], refs[n + i], refs[-1].at[i]) for i in range(n)]
    for copy in copies:
        copy.start()
    for copy in copies:
        copy.wait()


def per_device(n_site, corner, bcorner, edge, bedge, proj, joining, momentum):
    _, nb, m, kdim = edge.shape
    rows = m // HALVES
    nc = len(CHUNKS)
    tall = [rows * len(chunk[2]) for chunk in CHUNKS]
    n_near = n_site // 2
    bf = jnp.bfloat16
    hbm = pl.BlockSpec(memory_space=pl.ANY)
    smem = pl.BlockSpec(memory_space=pltpu.SMEM)
    vmem = pl.BlockSpec(memory_space=pltpu.VMEM)
    dma = pltpu.SemaphoreType.DMA
    results = pl.pallas_call(
        functools.partial(mega, n_site),
        out_shape=(
            jax.ShapeDtypeStruct(corner.shape, bf),
            jax.ShapeDtypeStruct(bcorner.shape, bf),
            jax.ShapeDtypeStruct((2, nb, m // n_site, m), jnp.float32),
        ),
        in_specs=[hbm, smem, hbm, hbm, hbm, hbm, hbm],
        out_specs=(vmem, vmem, vmem),
        scratch_shapes=[
            pltpu.VMEM((nb, m, kdim), bf),
            pltpu.VMEM((nb, m, kdim), bf),
            pltpu.VMEM((nb, kdim, m), bf),
            pltpu.VMEM((HALVES, 3, nb, rows, m), bf),
            pltpu.VMEM((nb, m, m), bf),
            pltpu.VMEM((nb, m, m), bf),
            pltpu.VMEM((8, m), jnp.float32),
            pltpu.VMEM((NX - 1, 8, m), jnp.float32),
            pltpu.VMEM((8, m), jnp.float32),
            pltpu.VMEM((NZ - 1, 8, m), jnp.float32),
            pltpu.VMEM((2, n_near, 2, nb // 2, 16, m), bf),
            pltpu.VMEM((2, n_near - 1, 2, nb // 2, 16, m), bf),
            pltpu.VMEM((2, nb // 2, 16, m), bf),
            pltpu.VMEM((2, nb // 2, 16, m), bf),
            pltpu.SMEM(((NX + 1 + 2 * NZ) * nb,), jnp.int32),
            pltpu.SMEM(joining.shape, jnp.int32),
        ]
        + [pltpu.VMEM((NZ * nb, t, m), bf) for t in tall]
        + [pltpu.VMEM((NZ, nb, t, m), bf) for t in tall for _ in range(5)]
        + [
            dma((3, nb)),
            dma((HALVES, 3)),
            dma((HALVES, 3)),
            dma((nc, NZ - 1)),
            dma((nc, NZ - 1)),
            dma((nc, NZ)),
            dma((nc, NX - 1)),
            dma((nc, NX - 1)),
            dma((nc, NZ)),
            dma((nc, NZ)),
            dma((nc, NZ)),
            dma((nc, NZ)),
            dma((2, NX - 1)),
            dma((2, NX - 1)),
            dma((2, n_near - 1)),
            dma((2, n_near - 1)),
            dma,
            dma,
            dma,
        ],
        compiler_params=pltpu.CompilerParams(
            collective_id=0, has_side_effects=True, vmem_limit_bytes=62 << 20
        ),
        name="column_move",
    )(joining, momentum, corner, bcorner, edge, bedge, proj)
    return pl.pallas_call(
        store,
        out_shape=tuple(jax.ShapeDtypeStruct(r.shape, r.dtype) for r in results),
        in_specs=[vmem] * len(results),
        out_specs=tuple(hbm for _ in results),
        scratch_shapes=[dma((len(results),))],
        name="store",
    )(*results)


def solution(mesh):
    in_specs = (
        P("site", "blk", None, None),
        P(None, "site", "blk", None, None),
        P("site", "blk", None, None),
        P("site", "blk", None, None),
        P("site", "blk", None, None),
        P("site", None),
        P(),
    )
    out_specs = (
        P("site", "blk", None, None),
        P(None, "site", "blk", None, None),
        P(None, "blk", "site", None),
    )
    return jax.shard_map(
        functools.partial(per_device, mesh.shape["site"]),
        mesh=mesh,
        in_specs=in_specs,
        out_specs=out_specs,
        check_vma=False,
    )
```

```python
import functools

import jax
import jax.numpy as jnp
from jax import lax
from jax.experimental import pallas as pl
from jax.experimental.pallas import tpu as pltpu
from jax.sharding import PartitionSpec as P

EPS = 1e-6
MESH = pl.DeviceIdType.MESH
NX = 4
NZ = 4
HALVES = 2
CHUNKS = (
    (False, 0, (2,), 0),
    (True, 0, (1,), 0),
    (False, 1, (1,), 1),
    (True, 1, (2,), 1),
    (False, 0, (0,), 2),
    (True, 1, (0,), 2),
)


def mega(
    n_site,
    join_ref,
    mom_ref,
    corner_ref,
    bcorner_ref,
    edge_ref,
    bedge_ref,
    proj_ref,
    outc_ref,
    outb_ref,
    sum_ref,
    edge_v,
    bedge_v,
    proj_v,
    cb_v,
    e_v,
    d_v,
    peak_src,
    peak_x,
    peak_mid,
    peak_z,
    msend,
    mrecv,
    mpart,
    mcross,
    tab,
    jsm,
    *rest,
):
    nb = edge_v.shape[0]
    m = cb_v.shape[-1]
    rows = m // HALVES
    nc = len(CHUNKS)
    along_z = [chunk[0] for chunk in CHUNKS]
    n_near = n_site // 2
    gath = rest[:nc]
    parts = [rest[nc + 5 * i : nc + 5 * i + 5] for i in range(nc)]
    (load_sem, s_send, s_recv, z_up, z_down, z_recv, x_send, x_recv, up_send, up_recv, dn_send, dn_recv, p_send, p_recv, m_send, m_recv, c_send, c_recv, j_sem) = rest[
        6 * nc :
    ]

    site = lax.axis_index("site")
    blk = lax.axis_index("blk")
    z = blk // NX
    x = blk % NX

    def at(s, b):
        return {"site": s, "blk": b}

    barrier = pltpu.get_barrier_semaphore()
    near, far = site % n_near, site // n_near

    def mate(k):
        return at(far * n_near + (near + k) % n_near, blk)

    def row_mate(dx):
        return at(site, z * NX + (x + dx) % NX)

    def column_mate(dz):
        return at(site, (z + dz) % NZ * NX + x)

    right, left = at((site + 1) % n_site, blk), at((site + n_site - 1) % n_site, blk)
    across = at((site + n_near) % n_site, blk)
    partners = (
        [right, left, across]
        + [mate(k) for k in range(1, n_near)]
        + [row_mate(d) for d in range(1, NX)]
        + [column_mate(d) for d in range(1, NZ)]
    )
    for partner in partners:
        pl.semaphore_signal(barrier, inc=1, device_id=partner, device_id_type=MESH)

    def loads(q):
        return [
            pltpu.make_async_copy(src.at[0, q], dst.at[q], load_sem.at[i, q])
            for i, (src, dst) in enumerate(((edge_ref, edge_v), (bedge_ref, bedge_v), (proj_ref, proj_v)))
        ]

    fetch = pltpu.make_async_copy(join_ref, jsm, j_sem)
    fetch.start()
    for q in range(nb):
        for copy in loads(q):
            copy.start()

    base = (NX + 1) * nb
    fetch.wait()
    for dx in range(NX):
        target = z * NX + (x + dx) % NX
        for k in range(nb):
            src = jsm[0, target * nb + k]
            dev = src // nb
            tab[dx * nb + k] = (dev // NX) * nb + (src - dev * nb)
            if dx == 0:
                tab[NX * nb + k] = (x - dev % NX + NX) % NX
    for t in range(NZ):
        for k in range(nb):
            src = jsm[0, (t * NX + x) * nb + k]
            dev = src // nb
            tab[base + t * nb + k] = (dev % NX) * nb + (src - dev * nb)
            tab[base + (NZ + t) * nb + k] = dev // NX

    pl.semaphore_wait(barrier, len(partners))

    def shift(h):
        part = pl.ds(h * rows, rows)
        sources = [corner_ref.at[0, :, part]] + [bcorner_ref.at[c, 0, :, part] for c in range(2)]
        return [
            pltpu.make_async_remote_copy(
                src_ref=source,
                dst_ref=cb_v.at[h, c],
                send_sem=s_send.at[h, c],
                recv_sem=s_recv.at[h, c],
                device_id=right,
                device_id_type=MESH,
            )
            for c, source in enumerate(sources)
        ]

    for h in range(HALVES):
        for copy in shift(h):
            copy.start()

    def local(q, carry):
        for copy in loads(q):
            copy.wait()
        both = jnp.concatenate([edge_v[q], bedge_v[q]], axis=0)
        prod = jnp.dot(both, proj_v[q], preferred_element_type=jnp.float32).astype(jnp.bfloat16)
        e_v[q] = prod[:m]
        d_v[q] = prod[m:]
        return carry

    lax.fori_loop(0, nb, local, 0)

    angle = jnp.full((8, m), mom_ref[0] * site.astype(jnp.float32), jnp.float32)
    cosine = jnp.cos(angle)[:1]
    sine = jnp.sin(angle)[:1]

    def join(h, top):
        for copy in shift(h):
            copy.wait_recv()

        def join_slot(q, top):
            left_rows = jnp.concatenate([cb_v[h, 0, q], cb_v[h, 1, q], cb_v[h, 2, q]], axis=0)
            main = jnp.dot(left_rows, e_v[q], preferred_element_type=jnp.float32)
            inserted = jnp.dot(cb_v[h, 0, q], d_v[q], preferred_element_type=jnp.float32)
            real, imag = main[rows : 2 * rows], main[2 * rows :]
            blocks = [
                main[:rows].astype(jnp.bfloat16),
                (cosine * real - sine * imag + inserted).astype(jnp.bfloat16),
                (sine * real + cosine * imag).astype(jnp.bfloat16),
            ]
            for c, (zfirst, half, held, _) in enumerate(CHUNKS):
                if half == h:
                    for i, b in enumerate(held):
                        gath[c][(z if zfirst else x) * nb + q, pl.ds(i * rows, rows)] = blocks[b]
            return jnp.maximum(top, jnp.max(jnp.abs(blocks[0].astype(jnp.float32))))

        return lax.fori_loop(0, nb, join_slot, top)

    peaks_x = [
        pltpu.make_async_remote_copy(
            src_ref=peak_src,
            dst_ref=peak_x.at[d - 1],
            send_sem=p_send.at[0, d - 1],
            recv_sem=p_recv.at[0, d - 1],
            device_id=row_mate(d),
            device_id_type=MESH,
        )
        for d in range(1, NX)
    ]
    peaks_z = [
        pltpu.make_async_remote_copy(
            src_ref=peak_mid,
            dst_ref=peak_z.at[d - 1],
            send_sem=p_send.at[1, d - 1],
            recv_sem=p_recv.at[1, d - 1],
            device_id=column_mate(d),
            device_id_type=MESH,
        )
        for d in range(1, NZ)
    ]

    def hop(c, j, up):
        sems = z_up if up else z_down
        step = z - j if up else j - z
        view = gath[c].at[pl.ds(j * nb, nb)]
        return pltpu.make_async_remote_copy(
            src_ref=view,
            dst_ref=view,
            send_sem=sems.at[c, step],
            recv_sem=z_recv.at[c, j],
            device_id=at(site, blk + NX if up else blk - NX),
            device_id_type=MESH,
        )

    def relay(c, s):
        @pl.when(z - s >= 0)
        def _():
            if s > 0:
                hop(c, z - s, True).wait_recv()

            if s < NZ - 1:

                @pl.when(z < NZ - 1)
                def _():
                    hop(c, z - s, True).start()

        @pl.when(z + s <= NZ - 1)
        def _():
            if s > 0:
                hop(c, z + s, False).wait_recv()

            if s < NZ - 1:

                @pl.when(z > 0)
                def _():
                    hop(c, z + s, False).start()

    def cross(c, dx):
        xsend, got = parts[c][:2]
        return pltpu.make_async_remote_copy(
            src_ref=xsend.at[dx - 1],
            dst_ref=got.at[dx],
            send_sem=x_send.at[c, dx - 1],
            recv_sem=x_recv.at[c, dx - 1],
            device_id=row_mate(dx),
            device_id_type=MESH,
        )

    def send_x(c):
        xsend, got = parts[c][:2]
        for dx in (2, 1, 3):
            for k in range(nb):
                xsend[dx - 1, k] = gath[c][tab[dx * nb + k]]
            cross(c, dx).start()
        for k in range(nb):
            got[0, k] = gath[c][tab[k]]

    def share(c, dx, owner):
        view = gath[c].at[pl.ds(owner * nb, nb)]
        return pltpu.make_async_remote_copy(
            src_ref=view,
            dst_ref=view,
            send_sem=x_send.at[c, dx - 1],
            recv_sem=x_recv.at[c, dx - 1],
            device_id=row_mate(dx),
            device_id_type=MESH,
        )

    def climb(c, t, up, last):
        out, inn, fin = parts[c][0 if up else 1], parts[c][2 if up else 3], parts[c][4]
        return pltpu.make_async_remote_copy(
            src_ref=out.at[t],
            dst_ref=fin.at[1 if up else 2] if last else inn.at[t],
            send_sem=(up_send if up else dn_send).at[c, t],
            recv_sem=(up_recv if up else dn_recv).at[c, t],
            device_id=at(site, blk + NX if up else blk - NX),
            device_id_type=MESH,
        )

    def flow(c, j, up):
        out, inn = parts[c][0 if up else 1], parts[c][2 if up else 3]
        first = j == (0 if up else NZ - 1)
        for t in range(NZ - 1, j, -1) if up else range(j):
            if not first:
                climb(c, t, up, False).wait_recv()
            for k in range(nb):
                mine = gath[c][tab[base + t * nb + k]]
                if not first:
                    mine = lax.select(tab[base + (NZ + t) * nb + k] == j, mine, inn[t, k])
                out[t, k] = mine
            climb(c, t, up, abs(t - j) == 1).start()

    def row_stage(c, stage):
        if stage == 0:
            for dx in (2, 1, 3):
                share(c, dx, x).start()
            return
        if stage == 1:
            for dx in (2, 1, 3):
                share(c, dx, (x + NX - dx) % NX).wait_recv()
        j = stage - 1
        if j < NZ - 1:

            @pl.when(z == j)
            def _():
                flow(c, j, True)

            @pl.when(z == NZ - 1 - j)
            def _():
                flow(c, NZ - 1 - j, False)

    def row_end(c):
        fin = parts[c][4]
        for k in range(nb):
            fin[0, k] = gath[c][tab[base + z * nb + k]]

        @pl.when(z > 0)
        def _():
            climb(c, z, True, True).wait_recv()

        @pl.when(z < NZ - 1)
        def _():
            climb(c, z, False, True).wait_recv()

    def picked(c, k):
        if along_z[c]:
            return parts[c][1][tab[NX * nb + k], k]
        source = tab[base + (NZ + z) * nb + k]
        which = jnp.where(source == z, 0, jnp.where(source < z, 1, 2))
        return parts[c][4][which, k]

    state = {}

    def finish(c):
        zfirst, h, blocks, _ = CHUNKS[c]
        if zfirst:
            for dx in (2, 1, 3):
                cross(c, dx).wait_recv()
        else:
            row_end(c)
        if "scale" not in state:
            best = peak_mid[...]
            for d, copy in enumerate(peaks_z):
                copy.wait_recv()
                best = jnp.maximum(best, peak_z[d])
            state["scale"] = best[:1] + EPS
        scale = state["scale"]
        held = {b: [] for b in blocks}
        for k in range(nb):
            value = picked(c, k).astype(jnp.float32) / scale
            for i, b in enumerate(blocks):
                block = value[i * rows : (i + 1) * rows]
                if b == 0:
                    outc_ref[0, k, pl.ds(h * rows, rows)] = block.astype(jnp.bfloat16)
                else:
                    outb_ref[b - 1, 0, k, pl.ds(h * rows, rows)] = block.astype(jnp.bfloat16)
                    held[b].append(block.reshape(rows // 8, 8, m))
        per = rows // 8
        for b in blocks:
            if b == 0:
                continue
            for j in range(nb // 2):
                pair = jnp.concatenate([held[b][2 * j], held[b][2 * j + 1]], axis=1).astype(jnp.bfloat16)
                for f in range(2):
                    lo, hi = max(h * per, f * n_near), min((h + 1) * per, (f + 1) * n_near)
                    if lo < hi:
                        msend[f, pl.ds(lo - f * n_near, hi - lo), b - 1, j] = pair[lo - h * per : hi - h * per]

    def spread(f, k):
        return pltpu.make_async_remote_copy(
            src_ref=msend.at[f, (near + k) % n_near],
            dst_ref=mrecv.at[f, k - 1],
            send_sem=m_send.at[f, k - 1],
            recv_sem=m_recv.at[f, k - 1],
            device_id=mate(k),
            device_id_type=MESH,
        )

    over = pltpu.make_async_remote_copy(
        src_ref=mpart,
        dst_ref=mcross,
        send_sem=c_send,
        recv_sem=c_recv,
        device_id=across,
        device_id_type=MESH,
    )

    def near_sum(f):
        total = msend[f, near].astype(jnp.float32)
        for k in range(1, n_near):
            spread(f, k).wait_recv()
            total = total + mrecv[f, k - 1].astype(jnp.float32)

        @pl.when(far == f)
        def _():
            for c in range(2):
                for j in range(nb // 2):
                    sum_ref[c, 2 * j] = total[c, j, :8]
                    sum_ref[c, 2 * j + 1] = total[c, j, 8:]

        @pl.when(far != f)
        def _():
            mpart[...] = total.astype(jnp.bfloat16)
            over.start()

    def far_sum():
        over.wait_recv()
        for c in range(2):
            for j in range(nb // 2):
                other = mcross[c, j].astype(jnp.float32)
                sum_ref[c, 2 * j] += other[:8]
                sum_ref[c, 2 * j + 1] += other[8:]

    last_b = [max(c for c in range(nc) if CHUNKS[c][1] == h and CHUNKS[c][2] != (0,)) for h in range(HALVES)]
    top = join(0, jnp.float32(0.0))
    for step in range(max(chunk[3] for chunk in CHUNKS) + NZ + 1):
        if step == 1:
            top = join(1, top)
            peak_src[...] = jnp.full(peak_src.shape, top, jnp.float32)
            for copy in peaks_x:
                copy.start()
        for c in range(nc):
            stage = step - CHUNKS[c][3]
            if 0 <= stage < NZ:
                if along_z[c]:
                    relay(c, stage)
                    if stage == NZ - 1:
                        send_x(c)
                else:
                    row_stage(c, stage)
        for c in range(nc):
            stage = step - CHUNKS[c][3]
            if stage == NZ:
                if c == nc - 1:
                    near_sum(1)
                finish(c)
                for f in range(HALVES):
                    if c == last_b[f]:
                        for k in (4, 3, 5, 2, 6, 1, 7):
                            spread(f, k).start()
                if c == last_b[1]:
                    near_sum(0)
        if step == 2:
            best = peak_src[...]
            for d, copy in enumerate(peaks_x):
                copy.wait_recv()
                best = jnp.maximum(best, peak_x[d])
            peak_mid[...] = best
            for copy in peaks_z:
                copy.start()
    far_sum()

    for h in range(HALVES):
        for copy in shift(h):
            copy.wait_send()
    for copy in peaks_x + peaks_z:
        copy.wait_send()
    for c in range(nc):
        if not along_z[c]:
            for dx in (1, 2, 3):
                share(c, dx, x).wait_send()
            for t in range(NZ):

                @pl.when(z < t)
                def _():
                    climb(c, t, True, False).wait_send()

                @pl.when(z > t)
                def _():
                    climb(c, t, False, False).wait_send()

            continue
        for s in range(NZ - 1):

            @pl.when(jnp.logical_and(z - s >= 0, z < NZ - 1))
            def _():
                hop(c, z - s, True).wait_send()

            @pl.when(jnp.logical_and(z + s <= NZ - 1, z > 0))
            def _():
                hop(c, z + s, False).wait_send()

        for dx in (1, 2, 3):
            cross(c, dx).wait_send()
    for f in range(HALVES):
        for k in range(1, n_near):
            spread(f, k).wait_send()
    over.wait_send()


def store(*refs):
    n = (len(refs) - 1) // 2
    copies = [pltpu.make_async_copy(refs[i], refs[n + i], refs[-1].at[i]) for i in range(n)]
    for copy in copies:
        copy.start()
    for copy in copies:
        copy.wait()


def per_device(n_site, corner, bcorner, edge, bedge, proj, joining, momentum):
    _, nb, m, kdim = edge.shape
    rows = m // HALVES
    nc = len(CHUNKS)
    tall = [rows * len(chunk[2]) for chunk in CHUNKS]
    n_near = n_site // 2
    bf = jnp.bfloat16
    hbm = pl.BlockSpec(memory_space=pl.ANY)
    smem = pl.BlockSpec(memory_space=pltpu.SMEM)
    vmem = pl.BlockSpec(memory_space=pltpu.VMEM)
    dma = pltpu.SemaphoreType.DMA
    results = pl.pallas_call(
        functools.partial(mega, n_site),
        out_shape=(
            jax.ShapeDtypeStruct(corner.shape, bf),
            jax.ShapeDtypeStruct(bcorner.shape, bf),
            jax.ShapeDtypeStruct((2, nb, m // n_site, m), jnp.float32),
        ),
        in_specs=[hbm, smem, hbm, hbm, hbm, hbm, hbm],
        out_specs=(vmem, vmem, vmem),
        scratch_shapes=[
            pltpu.VMEM((nb, m, kdim), bf),
            pltpu.VMEM((nb, m, kdim), bf),
            pltpu.VMEM((nb, kdim, m), bf),
            pltpu.VMEM((HALVES, 3, nb, rows, m), bf),
            pltpu.VMEM((nb, m, m), bf),
            pltpu.VMEM((nb, m, m), bf),
            pltpu.VMEM((8, m), jnp.float32),
            pltpu.VMEM((NX - 1, 8, m), jnp.float32),
            pltpu.VMEM((8, m), jnp.float32),
            pltpu.VMEM((NZ - 1, 8, m), jnp.float32),
            pltpu.VMEM((2, n_near, 2, nb // 2, 16, m), bf),
            pltpu.VMEM((2, n_near - 1, 2, nb // 2, 16, m), bf),
            pltpu.VMEM((2, nb // 2, 16, m), bf),
            pltpu.VMEM((2, nb // 2, 16, m), bf),
            pltpu.SMEM(((NX + 1 + 2 * NZ) * nb,), jnp.int32),
            pltpu.SMEM(joining.shape, jnp.int32),
        ]
        + [pltpu.VMEM((NZ * nb, t, m), bf) for t in tall]
        + [pltpu.VMEM((NZ, nb, t, m), bf) for t in tall for _ in range(5)]
        + [
            dma((3, nb)),
            dma((HALVES, 3)),
            dma((HALVES, 3)),
            dma((nc, NZ - 1)),
            dma((nc, NZ - 1)),
            dma((nc, NZ)),
            dma((nc, NX - 1)),
            dma((nc, NX - 1)),
            dma((nc, NZ)),
            dma((nc, NZ)),
            dma((nc, NZ)),
            dma((nc, NZ)),
            dma((2, NX - 1)),
            dma((2, NX - 1)),
            dma((2, n_near - 1)),
            dma((2, n_near - 1)),
            dma,
            dma,
            dma,
        ],
        compiler_params=pltpu.CompilerParams(
            collective_id=0, has_side_effects=True, vmem_limit_bytes=62 << 20
        ),
        name="column_move",
    )(joining, momentum, corner, bcorner, edge, bedge, proj)
    return pl.pallas_call(
        store,
        out_shape=tuple(jax.ShapeDtypeStruct(r.shape, r.dtype) for r in results),
        in_specs=[vmem] * len(results),
        out_specs=tuple(hbm for _ in results),
        scratch_shapes=[dma((len(results),))],
        name="store",
    )(*results)


def solution(mesh):
    in_specs = (
        P("site", "blk", None, None),
        P(None, "site", "blk", None, None),
        P("site", "blk", None, None),
        P("site", "blk", None, None),
        P("site", "blk", None, None),
        P("site", None),
        P(),
    )
    out_specs = (
        P("site", "blk", None, None),
        P(None, "site", "blk", None, None),
        P(None, "blk", "site", None),
    )
    return jax.shard_map(
        functools.partial(per_device, mesh.shape["site"]),
        mesh=mesh,
        in_specs=in_specs,
        out_specs=out_specs,
        check_vma=False,
    )
```

```python
import functools

import jax
import jax.numpy as jnp
from jax import lax
from jax.experimental import pallas as pl
from jax.experimental.pallas import tpu as pltpu
from jax.sharding import PartitionSpec as P

EPS = 1e-6
MESH = pl.DeviceIdType.MESH
NX = 4
NZ = 4
HALVES = 2
CHUNKS = (
    (False, 0, (2,), 0),
    (True, 0, (1,), 0),
    (True, 1, (2,), 1),
    (False, 1, (1,), 1),
    (False, 0, (0,), 2),
    (True, 1, (0,), 2),
)


def mega(
    n_site,
    join_ref,
    mom_ref,
    corner_ref,
    bcorner_ref,
    edge_ref,
    bedge_ref,
    proj_ref,
    outc_ref,
    outb_ref,
    sum_ref,
    edge_v,
    bedge_v,
    proj_v,
    cb_v,
    e_v,
    d_v,
    peak_src,
    peak_x,
    peak_mid,
    peak_z,
    msend,
    mrecv,
    mpart,
    mcross,
    tab,
    jsm,
    *rest,
):
    nb = edge_v.shape[0]
    m = cb_v.shape[-1]
    rows = m // HALVES
    nc = len(CHUNKS)
    along_z = [chunk[0] for chunk in CHUNKS]
    n_near = n_site // 2
    gath = rest[:nc]
    parts = [rest[nc + 5 * i : nc + 5 * i + 5] for i in range(nc)]
    (load_sem, s_send, s_recv, z_up, z_down, z_recv, x_send, x_recv, up_send, up_recv, dn_send, dn_recv, p_send, p_recv, m_send, m_recv, c_send, c_recv, j_sem) = rest[
        6 * nc :
    ]

    site = lax.axis_index("site")
    blk = lax.axis_index("blk")
    z = blk // NX
    x = blk % NX

    def at(s, b):
        return {"site": s, "blk": b}

    barrier = pltpu.get_barrier_semaphore()
    near, far = site % n_near, site // n_near

    def mate(k):
        return at(far * n_near + (near + k) % n_near, blk)

    def row_mate(dx):
        return at(site, z * NX + (x + dx) % NX)

    def column_mate(dz):
        return at(site, (z + dz) % NZ * NX + x)

    right, left = at((site + 1) % n_site, blk), at((site + n_site - 1) % n_site, blk)
    across = at((site + n_near) % n_site, blk)
    partners = (
        [right, left, across]
        + [mate(k) for k in range(1, n_near)]
        + [row_mate(d) for d in range(1, NX)]
        + [column_mate(d) for d in range(1, NZ)]
    )
    for partner in partners:
        pl.semaphore_signal(barrier, inc=1, device_id=partner, device_id_type=MESH)

    def loads(q):
        return [
            pltpu.make_async_copy(src.at[0, q], dst.at[q], load_sem.at[i, q])
            for i, (src, dst) in enumerate(((edge_ref, edge_v), (bedge_ref, bedge_v), (proj_ref, proj_v)))
        ]

    fetch = pltpu.make_async_copy(join_ref, jsm, j_sem)
    fetch.start()
    for q in range(nb):
        for copy in loads(q):
            copy.start()

    base = (NX + 1) * nb
    fetch.wait()
    for dx in range(NX):
        target = z * NX + (x + dx) % NX
        for k in range(nb):
            src = jsm[0, target * nb + k]
            dev = src // nb
            tab[dx * nb + k] = (dev // NX) * nb + (src - dev * nb)
            if dx == 0:
                tab[NX * nb + k] = (x - dev % NX + NX) % NX
    for t in range(NZ):
        for k in range(nb):
            src = jsm[0, (t * NX + x) * nb + k]
            dev = src // nb
            tab[base + t * nb + k] = (dev % NX) * nb + (src - dev * nb)
            tab[base + (NZ + t) * nb + k] = dev // NX

    pl.semaphore_wait(barrier, len(partners))

    def shift(h):
        part = pl.ds(h * rows, rows)
        sources = [corner_ref.at[0, :, part]] + [bcorner_ref.at[c, 0, :, part] for c in range(2)]
        return [
            pltpu.make_async_remote_copy(
                src_ref=source,
                dst_ref=cb_v.at[h, c],
                send_sem=s_send.at[h, c],
                recv_sem=s_recv.at[h, c],
                device_id=right,
                device_id_type=MESH,
            )
            for c, source in enumerate(sources)
        ]

    for h in range(HALVES):
        for copy in shift(h):
            copy.start()

    def local(q, carry):
        for copy in loads(q):
            copy.wait()
        both = jnp.concatenate([edge_v[q], bedge_v[q]], axis=0)
        prod = jnp.dot(both, proj_v[q], preferred_element_type=jnp.float32).astype(jnp.bfloat16)
        e_v[q] = prod[:m]
        d_v[q] = prod[m:]
        return carry

    lax.fori_loop(0, nb, local, 0)

    angle = jnp.full((8, m), mom_ref[0] * site.astype(jnp.float32), jnp.float32)
    cosine = jnp.cos(angle)[:1]
    sine = jnp.sin(angle)[:1]

    def join(h, top):
        for copy in shift(h):
            copy.wait_recv()

        def join_slot(q, top):
            left_rows = jnp.concatenate([cb_v[h, 0, q], cb_v[h, 1, q], cb_v[h, 2, q]], axis=0)
            main = jnp.dot(left_rows, e_v[q], preferred_element_type=jnp.float32)
            inserted = jnp.dot(cb_v[h, 0, q], d_v[q], preferred_element_type=jnp.float32)
            real, imag = main[rows : 2 * rows], main[2 * rows :]
            blocks = [
                main[:rows].astype(jnp.bfloat16),
                (cosine * real - sine * imag + inserted).astype(jnp.bfloat16),
                (sine * real + cosine * imag).astype(jnp.bfloat16),
            ]
            for c, (zfirst, half, held, _) in enumerate(CHUNKS):
                if half == h:
                    for i, b in enumerate(held):
                        gath[c][(z if zfirst else x) * nb + q, pl.ds(i * rows, rows)] = blocks[b]
            return jnp.maximum(top, jnp.max(jnp.abs(blocks[0].astype(jnp.float32))))

        return lax.fori_loop(0, nb, join_slot, top)

    peaks_x = [
        pltpu.make_async_remote_copy(
            src_ref=peak_src,
            dst_ref=peak_x.at[d - 1],
            send_sem=p_send.at[0, d - 1],
            recv_sem=p_recv.at[0, d - 1],
            device_id=row_mate(d),
            device_id_type=MESH,
        )
        for d in range(1, NX)
    ]
    peaks_z = [
        pltpu.make_async_remote_copy(
            src_ref=peak_mid,
            dst_ref=peak_z.at[d - 1],
            send_sem=p_send.at[1, d - 1],
            recv_sem=p_recv.at[1, d - 1],
            device_id=column_mate(d),
            device_id_type=MESH,
        )
        for d in range(1, NZ)
    ]

    def hop(c, j, up):
        sems = z_up if up else z_down
        step = z - j if up else j - z
        view = gath[c].at[pl.ds(j * nb, nb)]
        return pltpu.make_async_remote_copy(
            src_ref=view,
            dst_ref=view,
            send_sem=sems.at[c, step],
            recv_sem=z_recv.at[c, j],
            device_id=at(site, blk + NX if up else blk - NX),
            device_id_type=MESH,
        )

    def relay(c, s):
        @pl.when(z - s >= 0)
        def _():
            if s > 0:
                hop(c, z - s, True).wait_recv()

            if s < NZ - 1:

                @pl.when(z < NZ - 1)
                def _():
                    hop(c, z - s, True).start()

        @pl.when(z + s <= NZ - 1)
        def _():
            if s > 0:
                hop(c, z + s, False).wait_recv()

            if s < NZ - 1:

                @pl.when(z > 0)
                def _():
                    hop(c, z + s, False).start()

    def cross(c, dx):
        xsend, got = parts[c][:2]
        return pltpu.make_async_remote_copy(
            src_ref=xsend.at[dx - 1],
            dst_ref=got.at[dx],
            send_sem=x_send.at[c, dx - 1],
            recv_sem=x_recv.at[c, dx - 1],
            device_id=row_mate(dx),
            device_id_type=MESH,
        )

    def send_x(c):
        xsend, got = parts[c][:2]
        for dx in (2, 1, 3):
            for k in range(nb):
                xsend[dx - 1, k] = gath[c][tab[dx * nb + k]]
            cross(c, dx).start()
        for k in range(nb):
            got[0, k] = gath[c][tab[k]]

    def share(c, dx, owner):
        view = gath[c].at[pl.ds(owner * nb, nb)]
        return pltpu.make_async_remote_copy(
            src_ref=view,
            dst_ref=view,
            send_sem=x_send.at[c, dx - 1],
            recv_sem=x_recv.at[c, dx - 1],
            device_id=row_mate(dx),
            device_id_type=MESH,
        )

    def climb(c, t, up, last):
        out, inn, fin = parts[c][0 if up else 1], parts[c][2 if up else 3], parts[c][4]
        return pltpu.make_async_remote_copy(
            src_ref=out.at[t],
            dst_ref=fin.at[1 if up else 2] if last else inn.at[t],
            send_sem=(up_send if up else dn_send).at[c, t],
            recv_sem=(up_recv if up else dn_recv).at[c, t],
            device_id=at(site, blk + NX if up else blk - NX),
            device_id_type=MESH,
        )

    def flow(c, j, up):
        out, inn = parts[c][0 if up else 1], parts[c][2 if up else 3]
        first = j == (0 if up else NZ - 1)
        for t in range(NZ - 1, j, -1) if up else range(j):
            if not first:
                climb(c, t, up, False).wait_recv()
            for k in range(nb):
                mine = gath[c][tab[base + t * nb + k]]
                if not first:
                    mine = lax.select(tab[base + (NZ + t) * nb + k] == j, mine, inn[t, k])
                out[t, k] = mine
            climb(c, t, up, abs(t - j) == 1).start()

    def row_stage(c, stage):
        if stage == 0:
            for dx in (2, 1, 3):
                share(c, dx, x).start()
            return
        if stage == 1:
            for dx in (2, 1, 3):
                share(c, dx, (x + NX - dx) % NX).wait_recv()
        j = stage - 1
        if j < NZ - 1:

            @pl.when(z == j)
            def _():
                flow(c, j, True)

            @pl.when(z == NZ - 1 - j)
            def _():
                flow(c, NZ - 1 - j, False)

    def row_end(c):
        fin = parts[c][4]
        for k in range(nb):
            fin[0, k] = gath[c][tab[base + z * nb + k]]

        @pl.when(z > 0)
        def _():
            climb(c, z, True, True).wait_recv()

        @pl.when(z < NZ - 1)
        def _():
            climb(c, z, False, True).wait_recv()

    def picked(c, k):
        if along_z[c]:
            return parts[c][1][tab[NX * nb + k], k]
        source = tab[base + (NZ + z) * nb + k]
        which = jnp.where(source == z, 0, jnp.where(source < z, 1, 2))
        return parts[c][4][which, k]

    state = {}

    def finish(c):
        zfirst, h, blocks, _ = CHUNKS[c]
        if zfirst:
            for dx in (2, 1, 3):
                cross(c, dx).wait_recv()
        else:
            row_end(c)
        if "scale" not in state:
            best = peak_mid[...]
            for d, copy in enumerate(peaks_z):
                copy.wait_recv()
                best = jnp.maximum(best, peak_z[d])
            state["scale"] = best[:1] + EPS
        scale = state["scale"]
        held = {b: [] for b in blocks}
        for k in range(nb):
            value = picked(c, k).astype(jnp.float32) / scale
            for i, b in enumerate(blocks):
                block = value[i * rows : (i + 1) * rows]
                if b == 0:
                    outc_ref[0, k, pl.ds(h * rows, rows)] = block.astype(jnp.bfloat16)
                else:
                    outb_ref[b - 1, 0, k, pl.ds(h * rows, rows)] = block.astype(jnp.bfloat16)
                    held[b].append(block.reshape(rows // 8, 8, m))
        per = rows // 8
        for b in blocks:
            if b == 0:
                continue
            for j in range(nb // 2):
                pair = jnp.concatenate([held[b][2 * j], held[b][2 * j + 1]], axis=1).astype(jnp.bfloat16)
                for f in range(2):
                    lo, hi = max(h * per, f * n_near), min((h + 1) * per, (f + 1) * n_near)
                    if lo < hi:
                        msend[f, pl.ds(lo - f * n_near, hi - lo), b - 1, j] = pair[lo - h * per : hi - h * per]

    def spread(f, k):
        return pltpu.make_async_remote_copy(
            src_ref=msend.at[f, (near + k) % n_near],
            dst_ref=mrecv.at[f, k - 1],
            send_sem=m_send.at[f, k - 1],
            recv_sem=m_recv.at[f, k - 1],
            device_id=mate(k),
            device_id_type=MESH,
        )

    over = pltpu.make_async_remote_copy(
        src_ref=mpart,
        dst_ref=mcross,
        send_sem=c_send,
        recv_sem=c_recv,
        device_id=across,
        device_id_type=MESH,
    )

    def near_sum(f):
        total = msend[f, near].astype(jnp.float32)
        for k in range(1, n_near):
            spread(f, k).wait_recv()
            total = total + mrecv[f, k - 1].astype(jnp.float32)

        @pl.when(far == f)
        def _():
            for c in range(2):
                for j in range(nb // 2):
                    sum_ref[c, 2 * j] = total[c, j, :8]
                    sum_ref[c, 2 * j + 1] = total[c, j, 8:]

        @pl.when(far != f)
        def _():
            mpart[...] = total.astype(jnp.bfloat16)
            over.start()

    def far_sum():
        over.wait_recv()
        for c in range(2):
            for j in range(nb // 2):
                other = mcross[c, j].astype(jnp.float32)
                sum_ref[c, 2 * j] += other[:8]
                sum_ref[c, 2 * j + 1] += other[8:]

    last_b = [max(c for c in range(nc) if CHUNKS[c][1] == h and CHUNKS[c][2] != (0,)) for h in range(HALVES)]
    top = join(0, jnp.float32(0.0))
    for step in range(max(chunk[3] for chunk in CHUNKS) + NZ + 1):
        if step == 1:
            top = join(1, top)
            peak_src[...] = jnp.full(peak_src.shape, top, jnp.float32)
            for copy in peaks_x:
                copy.start()
        for c in range(nc):
            stage = step - CHUNKS[c][3]
            if 0 <= stage < NZ:
                if along_z[c]:
                    relay(c, stage)
                    if stage == NZ - 1:
                        send_x(c)
                else:
                    row_stage(c, stage)
        for c in range(nc):
            stage = step - CHUNKS[c][3]
            if stage == NZ:
                if c == nc - 1:
                    near_sum(1)
                finish(c)
                for f in range(HALVES):
                    if c == last_b[f]:
                        for k in (4, 3, 5, 2, 6, 1, 7):
                            spread(f, k).start()
                if c == last_b[1]:
                    near_sum(0)
        if step == 2:
            best = peak_src[...]
            for d, copy in enumerate(peaks_x):
                copy.wait_recv()
                best = jnp.maximum(best, peak_x[d])
            peak_mid[...] = best
            for copy in peaks_z:
                copy.start()
    far_sum()

    for h in range(HALVES):
        for copy in shift(h):
            copy.wait_send()
    for copy in peaks_x + peaks_z:
        copy.wait_send()
    for c in range(nc):
        if not along_z[c]:
            for dx in (1, 2, 3):
                share(c, dx, x).wait_send()
            for t in range(NZ):

                @pl.when(z < t)
                def _():
                    climb(c, t, True, False).wait_send()

                @pl.when(z > t)
                def _():
                    climb(c, t, False, False).wait_send()

            continue
        for s in range(NZ - 1):

            @pl.when(jnp.logical_and(z - s >= 0, z < NZ - 1))
            def _():
                hop(c, z - s, True).wait_send()

            @pl.when(jnp.logical_and(z + s <= NZ - 1, z > 0))
            def _():
                hop(c, z + s, False).wait_send()

        for dx in (1, 2, 3):
            cross(c, dx).wait_send()
    for f in range(HALVES):
        for k in range(1, n_near):
            spread(f, k).wait_send()
    over.wait_send()


def store(*refs):
    n = (len(refs) - 1) // 2
    copies = [pltpu.make_async_copy(refs[i], refs[n + i], refs[-1].at[i]) for i in range(n)]
    for copy in copies:
        copy.start()
    for copy in copies:
        copy.wait()


def per_device(n_site, corner, bcorner, edge, bedge, proj, joining, momentum):
    _, nb, m, kdim = edge.shape
    rows = m // HALVES
    nc = len(CHUNKS)
    tall = [rows * len(chunk[2]) for chunk in CHUNKS]
    n_near = n_site // 2
    bf = jnp.bfloat16
    hbm = pl.BlockSpec(memory_space=pl.ANY)
    smem = pl.BlockSpec(memory_space=pltpu.SMEM)
    vmem = pl.BlockSpec(memory_space=pltpu.VMEM)
    dma = pltpu.SemaphoreType.DMA
    results = pl.pallas_call(
        functools.partial(mega, n_site),
        out_shape=(
            jax.ShapeDtypeStruct(corner.shape, bf),
            jax.ShapeDtypeStruct(bcorner.shape, bf),
            jax.ShapeDtypeStruct((2, nb, m // n_site, m), jnp.float32),
        ),
        in_specs=[hbm, smem, hbm, hbm, hbm, hbm, hbm],
        out_specs=(vmem, vmem, vmem),
        scratch_shapes=[
            pltpu.VMEM((nb, m, kdim), bf),
            pltpu.VMEM((nb, m, kdim), bf),
            pltpu.VMEM((nb, kdim, m), bf),
            pltpu.VMEM((HALVES, 3, nb, rows, m), bf),
            pltpu.VMEM((nb, m, m), bf),
            pltpu.VMEM((nb, m, m), bf),
            pltpu.VMEM((8, m), jnp.float32),
            pltpu.VMEM((NX - 1, 8, m), jnp.float32),
            pltpu.VMEM((8, m), jnp.float32),
            pltpu.VMEM((NZ - 1, 8, m), jnp.float32),
            pltpu.VMEM((2, n_near, 2, nb // 2, 16, m), bf),
            pltpu.VMEM((2, n_near - 1, 2, nb // 2, 16, m), bf),
            pltpu.VMEM((2, nb // 2, 16, m), bf),
            pltpu.VMEM((2, nb // 2, 16, m), bf),
            pltpu.SMEM(((NX + 1 + 2 * NZ) * nb,), jnp.int32),
            pltpu.SMEM(joining.shape, jnp.int32),
        ]
        + [pltpu.VMEM((NZ * nb, t, m), bf) for t in tall]
        + [pltpu.VMEM((NZ, nb, t, m), bf) for t in tall for _ in range(5)]
        + [
            dma((3, nb)),
            dma((HALVES, 3)),
            dma((HALVES, 3)),
            dma((nc, NZ - 1)),
            dma((nc, NZ - 1)),
            dma((nc, NZ)),
            dma((nc, NX - 1)),
            dma((nc, NX - 1)),
            dma((nc, NZ)),
            dma((nc, NZ)),
            dma((nc, NZ)),
            dma((nc, NZ)),
            dma((2, NX - 1)),
            dma((2, NX - 1)),
            dma((2, n_near - 1)),
            dma((2, n_near - 1)),
            dma,
            dma,
            dma,
        ],
        compiler_params=pltpu.CompilerParams(
            collective_id=0, has_side_effects=True, vmem_limit_bytes=62 << 20
        ),
        name="column_move",
    )(joining, momentum, corner, bcorner, edge, bedge, proj)
    return pl.pallas_call(
        store,
        out_shape=tuple(jax.ShapeDtypeStruct(r.shape, r.dtype) for r in results),
        in_specs=[vmem] * len(results),
        out_specs=tuple(hbm for _ in results),
        scratch_shapes=[dma((len(results),))],
        name="store",
    )(*results)


def solution(mesh):
    in_specs = (
        P("site", "blk", None, None),
        P(None, "site", "blk", None, None),
        P("site", "blk", None, None),
        P("site", "blk", None, None),
        P("site", "blk", None, None),
        P("site", None),
        P(),
    )
    out_specs = (
        P("site", "blk", None, None),
        P(None, "site", "blk", None, None),
        P(None, "blk", "site", None),
    )
    return jax.shard_map(
        functools.partial(per_device, mesh.shape["site"]),
        mesh=mesh,
        in_specs=in_specs,
        out_specs=out_specs,
        check_vma=False,
    )
```
